32 devices in a mesh: vol: 2 (over y), gz: 16 (over z, x, core).
Axes of the slice: x: 2, y: 2, z: 4, core: 2. Of those that a mesh axis runs over, the one named last changes fastest.
Arguments:
- volume: bfloat16 [2, 32, 64, 64, 128], P('vol', None, 'gz'), may hold values from -6 to 6
- kernel: bfloat16 [64, 32, 3, 3, 3], replicated, may hold values from -0.21875 to 0.21875
- cotangent: bfloat16 [2, 64, 32, 32, 64], P('vol', None, None, 'gz'), may hold values from -6 to 6
Outputs:
- features: bfloat16 [2, 64, 32, 32, 64], P('vol', None, None, 'gz')
- volume_grad: bfloat16 [2, 32, 64, 64, 128], P('vol', None, 'gz')
- kernel_grad: float32 [64, 32, 3, 3, 3], replicated
The draws below stay inside these ranges and needn't reach their ends.
All inputs are finite; a program needn't handle non-finite values.
Results may differ from the reference program's by a relative error of at most 0.004.
Values may be sent and summed in bfloat16 or wider, within the bound.
No kernel may reach another device: no remote copies, remote signals or barrier semaphores. Data moves between devices by JAX's collectives and lax.ppermute only.
A program may use at most 192 MiB of HBM per device.

```python
import jax
import jax.numpy as jnp
from jax import lax

CIN = 32
COUT = 64
Y = 64
X = 128
VOLUMES = 2
Z = 64
OZ = 32
OY = 32
OX = 64


def level_of(own_key, shape, pieces, least, high):
    loudness, own = 1.0, jax.random.fold_in(own_key, 6)
    for position, parts in pieces:
        heights = jnp.exp(jax.random.uniform(jax.random.fold_in(own, position), (parts,), jnp.float32, least / len(pieces), high / len(pieces)))
        loudness = loudness * jnp.repeat(heights, shape[position] // parts).reshape([-1 if axis == position else 1 for axis in range(len(shape))])
    return loudness


def centred(key, shape, spread, reach, pieces=(), held_as=jnp.bfloat16):
    array = spread * jax.random.normal(key, shape, jnp.float32)
    if pieces:
        array = array * level_of(key, shape, pieces, -0.22, 0.18)
    return jnp.clip(array, -reach, reach).astype(held_as)


def setup_inputs(seed: int = 0) -> dict:
    seeds = jax.random.split(jax.random.key(seed), 4)
    volume = centred(seeds[0], (VOLUMES, CIN, Z, Y, X), 1.0, 6.0, ((0, 2), (2, 16)))
    kernel = centred(seeds[1], (COUT, CIN, 3, 3, 3), (CIN * 27) ** -0.5, 0.21875)
    cotangent = centred(seeds[2], (VOLUMES, COUT, OZ, OY, OX), 1.0, 6.0, ((0, 2), (3, 16)))
    return dict(volume=volume, kernel=kernel, cotangent=cotangent)


def convolve(volume_one, kernel_one):
    return lax.conv_general_dilated(volume_one[None], kernel_one, (2, 2, 2), ((1, 1), (1, 1), (1, 1)), dimension_numbers=('NCDHW', 'OIDHW', 'NCDHW'), precision=lax.Precision.HIGHEST)[0]

def reference(volume, kernel, cotangent):
    kernel_wide = kernel.astype(jnp.float32)

    def one_volume(carry, pair):
        volume_one, grads_one = pair
        output, pullback = jax.vjp(convolve, volume_one.astype(jnp.float32), kernel_wide)
        input_grad, weight_grad = pullback(grads_one.astype(jnp.float32))
        return (carry + weight_grad, (output.astype(jnp.bfloat16), input_grad.astype(jnp.bfloat16)))
    start = jnp.zeros(kernel.shape, jnp.float32)
    summed, (features, volume_grad) = lax.scan(one_volume, start, (volume, cotangent))
    return (features, volume_grad, summed / VOLUMES)
```

```python
import jax
import jax.numpy as jnp
from jax import lax
from jax.experimental import pallas as pl
from jax.experimental.pallas import tpu as pltpu
from jax.sharding import PartitionSpec as P

F32 = jnp.float32
BF16 = jnp.bfloat16
TAP = {(0, 0): 1, (0, 1): 2, (1, 1): 0, (1, 0): None}


def dot(a, b):
    return lax.dot_general(a, b, (((1,), (0,)), ((), ())), preferred_element_type=F32)


def dot_t(a, b):
    return lax.dot_general(a, b, (((1,), (1,)), ((), ())), preferred_element_type=F32)


def iota(shape, dim):
    return lax.broadcasted_iota(jnp.int32, shape, dim)


def split_matrix(x, swapped):
    shape = (2 * x, 2 * x)
    row, col = iota(shape, 0), iota(shape, 1)
    half_in, x_in = row // x, row % x
    parity, half_out, r = col // x, (col % x) // (x // 2), col % (x // 2)
    if swapped:
        half_out = 1 - half_out
    hit = (half_in == half_out) & (x_in == 2 * r + parity)
    return jnp.where(hit, 1.0, 0.0).astype(BF16)


def join_matrix(x):
    shape = (2 * x, 2 * x)
    row, col = iota(shape, 0), iota(shape, 1)
    half_in, x_in = col // x, col % x
    parity, half_out, r = row // x, (row % x) // (x // 2), row % (x // 2)
    hit = (half_in == half_out) & (x_in == 2 * r + parity)
    return jnp.where(hit, 1.0, 0.0).astype(BF16)


def weight_block(k_ref, a, b, xp):
    if a is None or b is None:
        return jnp.zeros((k_ref.shape[1], 2 * k_ref.shape[2]), BF16)
    at = (a * 3 + b) * 3
    if xp == 0:
        one = k_ref[at + 1]
        return jnp.concatenate([one, jnp.zeros_like(one)], axis=1)
    return jnp.concatenate([k_ref[at + 2], k_ref[at]], axis=1)


def forward_kernel(vol_ref, k_ref, v8_ref, send_ref, t_ref, x_ref, vs_ref, w_ref):
    cin, planes, ys, xs = vol_ref.shape
    cout = k_ref.shape[2]
    blocks = ys // 4
    quarter = 4 * cin
    for dp in range(2):
        cols = pl.ds(dp * 2 * cout, 2 * cout)
        for zp in range(2):
            for xp in range(2):
                for yp in range(2):
                    w_ref[pl.ds(((zp * 2 + yp) * 2 + xp) * cin, cin), cols] = weight_block(
                        k_ref, TAP[dp, zp], TAP[0, yp], xp
                    )
                w_ref[pl.ds(2 * quarter + (zp * 2 + xp) * cin, cin), cols] = weight_block(
                    k_ref, TAP[dp, zp], TAP[1, 1], xp
                )
    split = split_matrix(xs, False)
    split_swapped = split_matrix(xs, True)

    def prepare(z, carry):
        t_ref[...] = vol_ref[:, z].astype(F32).reshape(cin * ys, xs)
        for y in range(ys):
            k, h, yp = y // 4, (y // 2) % 2, y % 2
            rows = t_ref[pl.ds(y, cin, stride=ys), :]
            x_ref[yp, pl.ds(k * cin, cin), pl.ds(h * xs, xs)] = rows.astype(BF16)
        for yp in range(2):
            out = dot(x_ref[yp], split).astype(BF16)
            for k in range(blocks):
                for xp in range(2):
                    v8_ref[z, pl.ds((yp * 2 + xp) * cin, cin), pl.ds(k * xs, xs)] = out[
                        k * cin : (k + 1) * cin, xp * xs : (xp + 1) * xs
                    ]
        before = jnp.concatenate(
            [jnp.zeros((cin, xs), BF16), x_ref[1, : (blocks - 1) * cin, xs:]], axis=0
        )
        pair = jnp.concatenate([x_ref[1, :, :xs], before], axis=1)
        out = dot(pair, split_swapped).astype(BF16)
        for k in range(blocks):
            for xp in range(2):
                vs_ref[z, pl.ds(xp * cin, cin), pl.ds(k * xs, xs)] = out[
                    k * cin : (k + 1) * cin, xp * xs : (xp + 1) * xs
                ]
        return carry

    lax.fori_loop(0, planes, prepare, 0)
    weights = jnp.transpose(w_ref[...], (1, 0))
    group = 4
    width = group * xs
    first = iota((cout, width), 1) % (xs // 2) == 0

    def moved(value):
        return jnp.where(first, 0.0, pltpu.roll(value, 1, axis=1))

    def store(chunk, plane, value):
        value = value.astype(BF16)
        for kk in range(group):
            send_ref[chunk * group + kk, plane] = value[:, kk * xs : (kk + 1) * xs]

    def compute(chunk, carry):
        lanes = pl.ds(pl.multiple_of(chunk * width, width), width)
        left = None
        for p in range(planes // 2):
            rhs = jnp.concatenate(
                [
                    v8_ref[pl.ds(2 * p, 2), :, lanes].reshape(2 * quarter, width),
                    vs_ref[pl.ds(2 * p, 2), :, lanes].reshape(quarter, width),
                ],
                axis=0,
            )
            acc = dot(weights, rhs)
            here = acc[:cout] + moved(acc[cout : 2 * cout])
            after = acc[2 * cout : 3 * cout] + moved(acc[3 * cout :])
            store(chunk, p, here if left is None else here + left)
            left = after
        store(chunk, planes // 2, left)
        return carry

    lax.fori_loop(0, blocks // group, compute, 0)


def weight_kernel(recv_ref, v8_ref, gg_ref, part_ref):
    blocks, slots, cout, xs = recv_ref.shape
    planes, quarter, _ = v8_ref.shape
    cin = quarter // 4
    shape = (2 * xs, 3 * xs)
    row, col = iota(shape, 0), iota(shape, 1)
    variant, lane = col // xs + 1, col % xs
    dq, dr = variant // 2, variant % 2
    hit = (row == lane + dq * (xs // 2) + dr) & ((dr == 0) | (lane % (xs // 2) != xs // 2 - 1))
    shifts = jnp.where(hit, 1.0, 0.0).astype(BF16)

    def shifted(p, carry):
        here = recv_ref[:, p].reshape(blocks * cout, xs)
        after = jnp.concatenate([here[cout:], jnp.zeros((cout, xs), BF16)], axis=0)
        out = dot(jnp.concatenate([here, after], axis=1), shifts).astype(BF16)
        for k in range(blocks):
            lanes = pl.ds(k * xs, xs)
            rows = slice(k * cout, (k + 1) * cout)
            gg_ref[p, pl.ds(0, cout), lanes] = here[rows]
            for v in range(1, 4):
                gg_ref[p, pl.ds(v * cout, cout), lanes] = out[rows, (v - 1) * xs : v * xs]
        return carry

    lax.fori_loop(0, slots, shifted, 0)
    near, far = None, None
    for p in range(planes // 2):
        both = v8_ref[pl.ds(2 * p, 2)].reshape(2 * quarter, blocks * xs)
        one = dot_t(both, gg_ref[p])
        two = dot_t(v8_ref[2 * p + 1], gg_ref[p + 1])
        near = one if near is None else near + one
        far = two if far is None else far + two

    def piece(a, b, xp):
        dp, zp = [key for key, tap in TAP.items() if tap == a][0]
        dq, yp = [key for key, tap in TAP.items() if tap == b][0]
        at = (yp * 2 + xp) * cin
        if dp == 0:
            return near[zp * quarter + at : zp * quarter + at + cin, dq * 2 * cout : (dq + 1) * 2 * cout]
        return far[at : at + cin, dq * 2 * cout : (dq + 1) * 2 * cout]

    halves = []
    for a in range(3):
        for b in range(3):
            part_ref[pl.ds((a * 3 + b) * cin, cin), :] = piece(a, b, 1)
            halves.append(piece(a, b, 0)[:, :cout])
    halves.append(jnp.zeros((cin, cout), F32))
    for t in range(0, 10, 2):
        part_ref[pl.ds((9 + t // 2) * cin, cin), :] = jnp.concatenate(halves[t : t + 2], axis=1)
    rest = part_ref.shape[0] - 14 * cin
    if rest:
        part_ref[pl.ds(14 * cin, rest), :] = jnp.zeros((rest, 2 * cout), F32)


def input_kernel(gg_ref, k_ref, out_ref, w_ref, t_ref):
    cin, planes, ys, xs = out_ref.shape
    cout = k_ref.shape[2]
    blocks = ys // 4
    for zp in range(2):
        for yp in range(2):
            for xp in range(2):
                for dp in range(2):
                    for dq in range(2):
                        w_ref[
                            pl.ds(((zp * 2 + yp) * 2 + xp) * cin, cin),
                            pl.ds((dp * 2 + dq) * 2 * cout, 2 * cout),
                        ] = weight_block(k_ref, TAP[dp, zp], TAP[dq, yp], xp)
    join = join_matrix(xs)
    weights = w_ref[...]
    group = 4
    width = group * xs

    def one(p, carry):
        for chunk in range(blocks // group):
            lanes = pl.ds(chunk * width, width)
            rhs = gg_ref[pl.ds(p, 2), :, lanes].reshape(8 * cout, width)
            acc = dot(weights, rhs).astype(BF16)
            pairs = []
            for zy in range(4):
                even = acc[zy * 2 * cin : (zy * 2 + 1) * cin]
                odd = acc[(zy * 2 + 1) * cin : (zy * 2 + 2) * cin]
                for kk in range(group):
                    at = slice(kk * xs, (kk + 1) * xs)
                    pairs.append(jnp.concatenate([even[:, at], odd[:, at]], axis=1))
            joined = dot(jnp.concatenate(pairs, axis=0), join)
            for zy in range(4):
                for kk in range(group):
                    at = (zy * group + kk) * cin
                    for h in range(2):
                        y = 4 * (chunk * group + kk) + 2 * h + zy % 2
                        t_ref[zy // 2, pl.ds(y, cin, stride=ys), :] = joined[
                            at : at + cin, h * xs : (h + 1) * xs
                        ]
        for zp in range(2):
            out_ref[:, 2 * p + zp] = t_ref[zp].reshape(cin, ys, xs).astype(BF16)
        return carry

    lax.fori_loop(0, planes // 2, one, 0)


def final_kernel(sum_ref, out_ref, *, scale):
    _, cin, cout = out_ref.shape
    for t in range(9):
        full = sum_ref[pl.ds(t * cin, cin), :] * scale
        out_ref[3 * t + 2] = full[:, :cout]
        out_ref[3 * t] = full[:, cout:]
        half = sum_ref[pl.ds((9 + t // 2) * cin, cin), :] * scale
        out_ref[3 * t + 1] = half[:, (t % 2) * cout : (t % 2 + 1) * cout]


def call(kernel, outs, scratch=()):
    return pl.pallas_call(
        kernel,
        out_shape=outs,
        scratch_shapes=scratch,
        compiler_params=pltpu.CompilerParams(vmem_limit_bytes=48 << 20),
    )


def shards(volume, kernel, cotangent):
    count = lax.axis_size("gz")
    everyone = count * lax.axis_size("vol")
    _, cin, planes, ys, xs = volume.shape
    _, cout, ozs, band, oxs = cotangent.shape
    slots = planes // 2
    blocks = ys // 4
    lanes = blocks * xs
    taps = jnp.transpose(kernel, (2, 3, 4, 1, 0)).reshape(27, cin, cout)

    grads = jnp.transpose(cotangent[0], (1, 0, 2, 3)).reshape(count, slots, cout, band * oxs)
    above = jnp.concatenate([grads[1:, :1], jnp.zeros_like(grads[:1, :1])], axis=0)
    packed = jnp.concatenate([grads, above], axis=1)
    recv = lax.all_to_all(packed, "gz", 0, 0, tiled=True)
    if band != 2:
        recv = recv.reshape(blocks, 2, slots + 1, cout, oxs)
        recv = jnp.transpose(recv, (0, 2, 3, 1, 4)).reshape(blocks, slots + 1, cout, xs)

    v8, send = call(
        forward_kernel,
        (
            jax.ShapeDtypeStruct((planes, 4 * cin, lanes), BF16),
            jax.ShapeDtypeStruct((blocks, slots + 1, cout, xs), BF16),
        ),
        (
            pltpu.VMEM((cin * ys, xs), F32),
            pltpu.VMEM((2, blocks * cin, 2 * xs), BF16),
            pltpu.VMEM((planes, 2 * cin, lanes), BF16),
            pltpu.VMEM((12 * cin, 4 * cout), BF16),
        ),
    )(volume[0], taps)
    if band != 2:
        send = send.reshape(blocks, slots + 1, cout, 2, oxs)
        send = jnp.transpose(send, (0, 3, 1, 2, 4)).reshape(count, slots + 1, cout, band * oxs)
    back = lax.all_to_all(send, "gz", 0, 0, tiled=True)
    carried = jnp.concatenate([jnp.zeros_like(back[:1, slots:]), back[:-1, slots:]], axis=0)
    first = (back[:, :1].astype(F32) + carried.astype(F32)).astype(BF16)
    whole = jnp.concatenate([first, back[:, 1:slots]], axis=1)
    features = jnp.transpose(whole.reshape(ozs, cout, band, oxs), (1, 0, 2, 3))[None]

    rows = 14 * cin
    unit = 8 * everyone if rows >= 8 * everyone else everyone
    rows = -(-rows // unit) * unit
    gg, part = call(
        weight_kernel,
        (
            jax.ShapeDtypeStruct((slots + 1, 4 * cout, lanes), BF16),
            jax.ShapeDtypeStruct((rows, 2 * cout), F32),
        ),
    )(recv, v8)
    both = ("vol", "gz")
    spread = lax.all_to_all(part.reshape(everyone, rows // everyone, 2 * cout), both, 0, 0, tiled=True)
    total = jnp.sum(spread, axis=0)
    total = lax.all_to_all(jnp.broadcast_to(total, spread.shape), both, 0, 0, tiled=True)

    volume_grad = call(
        input_kernel,
        jax.ShapeDtypeStruct((cin, planes, ys, xs), BF16),
        (
            pltpu.VMEM((8 * cin, 8 * cout), BF16),
            pltpu.VMEM((2, cin * ys, xs), F32),
        ),
    )(gg, taps)[None]

    volumes = volume.shape[0] * lax.axis_size("vol")

    def finish(sum_ref, out_ref):
        final_kernel(sum_ref, out_ref, scale=1.0 / volumes)

    kernel_grad = call(finish, jax.ShapeDtypeStruct((27, cin, cout), F32))(
        total.reshape(rows, 2 * cout)
    )
    kernel_grad = jnp.transpose(kernel_grad.reshape(3, 3, 3, cin, cout), (4, 3, 0, 1, 2))
    return (features, volume_grad, kernel_grad)


def solution(mesh):
    placed = (P("vol", None, "gz", None, None), P(), P("vol", None, None, "gz", None))
    return jax.shard_map(
        shards,
        mesh=mesh,
        in_specs=placed,
        out_specs=(P("vol", None, None, "gz", None), P("vol", None, "gz", None, None), P()),
        check_vma=False,
    )
```

```python
import jax
import jax.numpy as jnp
from jax import lax
from jax.experimental import pallas as pl
from jax.experimental.pallas import tpu as pltpu
from jax.sharding import PartitionSpec as P


F32 = jnp.float32
BF16 = jnp.bfloat16
TAP = {(0, 0): 1, (0, 1): 2, (1, 1): 0, (1, 0): None}


def dot(a, b):
    return lax.dot_general(a, b, (((1,), (0,)), ((), ())), preferred_element_type=F32)


def dot_t(a, b):
    return lax.dot_general(a, b, (((1,), (1,)), ((), ())), preferred_element_type=F32)


def iota(shape, dim):
    return lax.broadcasted_iota(jnp.int32, shape, dim)


def tap_matrix(x, swapped):
    shape = (2 * x, 3 * x)
    row, col = iota(shape, 0), iota(shape, 1)
    half_in, x_in = row // x, row % x
    tap, half_out, r = col // x, (col % x) // (x // 2), col % (x // 2)
    if swapped:
        half_out = 1 - half_out
    hit = (half_in == half_out) & (x_in == 2 * r + tap - 1)
    return jnp.where(hit, 1.0, 0.0).astype(BF16)


def join_matrix(x):
    shape = (2 * x, 2 * x)
    row, col = iota(shape, 0), iota(shape, 1)
    half_in, x_in = col // x, col % x
    parity, half_out, r = row // x, (row % x) // (x // 2), row % (x // 2)
    hit = (half_in == half_out) & (x_in == 2 * r + parity)
    return jnp.where(hit, 1.0, 0.0).astype(BF16)


def shift_matrix(x):
    shape = (2 * x, 3 * x)
    row, col = iota(shape, 0), iota(shape, 1)
    variant, lane = col // x + 1, col % x
    dq, dr = variant // 2, variant % 2
    hit = (row == lane + dq * (x // 2) + dr) & ((dr == 0) | (lane % (x // 2) != x // 2 - 1))
    return jnp.where(hit, 1.0, 0.0).astype(BF16)


def weight_block(k_ref, a, b, xp):
    if a is None or b is None:
        return jnp.zeros((k_ref.shape[1], 2 * k_ref.shape[2]), BF16)
    at = (a * 3 + b) * 3
    if xp == 0:
        one = k_ref[at + 1]
        return jnp.concatenate([one, jnp.zeros_like(one)], axis=1)
    return jnp.concatenate([k_ref[at + 2], k_ref[at]], axis=1)


def forward_kernel(vol_ref, k_ref, xx_ref, send_ref, t_ref, x_ref):
    cin, planes, ys, xs = vol_ref.shape
    cout = k_ref.shape[2]
    blocks = ys // 4
    split = tap_matrix(xs, False)
    split_swapped = tap_matrix(xs, True)

    def prepare(z, carry):
        t_ref[...] = vol_ref[:, z].astype(F32).reshape(cin * ys, xs)
        for y in range(ys):
            k, h, yp = y // 4, (y // 2) % 2, y % 2
            rows = t_ref[pl.ds(y, cin, stride=ys), :]
            x_ref[yp, pl.ds(k * cin, cin), pl.ds(h * xs, xs)] = rows.astype(BF16)
        before = jnp.concatenate(
            [jnp.zeros((cin, xs), BF16), x_ref[1, : (blocks - 1) * cin, xs:]], axis=0
        )
        swapped = jnp.concatenate([x_ref[1, :, :xs], before], axis=1)
        for b, (pair, matrix) in enumerate(
            [(swapped, split_swapped), (x_ref[0], split), (x_ref[1], split)]
        ):
            out = dot(pair, matrix).astype(BF16)
            for k in range(blocks):
                for e in range(3):
                    xx_ref[z, pl.ds((b * 3 + e) * cin, cin), pl.ds(k * xs, xs)] = out[
                        k * cin : (k + 1) * cin, e * xs : (e + 1) * xs
                    ]
        return carry

    lax.fori_loop(0, planes, prepare, 0)
    w = k_ref[...].reshape(3, 9 * cin, cout)
    even = jnp.transpose(w[1], (1, 0))
    odd = jnp.transpose(jnp.concatenate([w[2], w[0]], axis=1), (1, 0))
    group = 4
    width = group * xs

    def store(chunk, plane, value):
        value = value.astype(BF16)
        for kk in range(group):
            send_ref[chunk * group + kk, plane] = value[:, kk * xs : (kk + 1) * xs]

    def compute(chunk, carry):
        lanes = pl.ds(pl.multiple_of(chunk * width, width), width)
        left = None
        for p in range(planes // 2):
            low = dot(even, xx_ref[2 * p, :, lanes])
            high = dot(odd, xx_ref[2 * p + 1, :, lanes])
            here = low + high[:cout]
            store(chunk, p, here if left is None else here + left)
            left = high[cout:]
        store(chunk, planes // 2, left)
        return carry

    lax.fori_loop(0, blocks // group, compute, 0)


def weight_kernel(recv_ref, xx_ref, send_ref, mix_ref):
    blocks, slots, _, xs = recv_ref.shape
    planes, rows, _ = xx_ref.shape
    count, feature_rows, _ = send_ref.shape
    unit = mix_ref.shape[1] - feature_rows
    for k in range(count):
        mix_ref[k, pl.ds(0, feature_rows), :] = send_ref[k]
    grads = [
        jnp.concatenate([recv_ref[k, p] for k in range(blocks)], axis=1) for p in range(slots)
    ]
    low, high = None, None
    for p in range(planes // 2):
        one = dot_t(xx_ref[2 * p], grads[p])
        two = dot_t(xx_ref[2 * p + 1], jnp.concatenate([grads[p], grads[p + 1]], axis=0))
        low = one if low is None else low + one
        high = two if high is None else high + two
    part = jnp.concatenate(
        [
            high,
            jnp.concatenate([low[: rows // 2], low[rows // 2 :]], axis=1),
            jnp.zeros((count * unit - rows - rows // 2, xs), F32),
        ],
        axis=0,
    ).astype(BF16)
    for k in range(count):
        mix_ref[k, pl.ds(feature_rows, unit), :] = part[k * unit : (k + 1) * unit]


def sum_kernel(back_ref, total_ref, *, scale):
    count, rows, _ = back_ref.shape
    everyone, unit, _ = total_ref.shape
    total = None
    for k in range(count):
        piece = back_ref[k, pl.ds(rows - unit, unit), :].astype(F32)
        total = piece if total is None else total + piece
    total = (total * scale).astype(BF16)
    for k in range(everyone):
        total_ref[k] = total


def final_kernel(total_ref, out_ref):
    _, rows, cout = out_ref.shape
    volumes, count, unit, xs = total_ref.shape
    total = total_ref[0].astype(F32)
    for v in range(1, volumes):
        total = total + total_ref[v].astype(F32)
    total = total.reshape(count * unit, xs)
    high = total[:rows]
    low = total[rows : rows + rows // 2]
    out_ref[2] = high[:, :cout]
    out_ref[0] = high[:, cout:]
    out_ref[1] = jnp.concatenate([low[:, :cout], low[:, cout:]], axis=0)


def input_kernel(recv_ref, k_ref, out_ref, gg_ref, w_ref, t_ref):
    cin, planes, ys, xs = out_ref.shape
    blocks, slots, cout, _ = recv_ref.shape
    shifts = shift_matrix(xs)

    def shifted(p, carry):
        here = recv_ref[:, p].reshape(blocks * cout, xs)
        after = jnp.concatenate([here[cout:], jnp.zeros((cout, xs), BF16)], axis=0)
        out = dot(jnp.concatenate([here, after], axis=1), shifts).astype(BF16)
        for k in range(blocks):
            lanes = pl.ds(k * xs, xs)
            rows = slice(k * cout, (k + 1) * cout)
            gg_ref[p, pl.ds(0, cout), lanes] = here[rows]
            for v in range(1, 4):
                gg_ref[p, pl.ds(v * cout, cout), lanes] = out[rows, (v - 1) * xs : v * xs]
        return carry

    lax.fori_loop(0, slots, shifted, 0)
    for zp in range(2):
        for yp in range(2):
            for xp in range(2):
                for dp in range(2):
                    for dq in range(2):
                        w_ref[
                            pl.ds(((zp * 2 + yp) * 2 + xp) * cin, cin),
                            pl.ds((dp * 2 + dq) * 2 * cout, 2 * cout),
                        ] = weight_block(k_ref, TAP[dp, zp], TAP[dq, yp], xp)
    join = join_matrix(xs)
    weights = w_ref[...]
    group = 4
    width = group * xs

    def one(p, carry):
        for chunk in range(blocks // group):
            lanes = pl.ds(chunk * width, width)
            rhs = gg_ref[pl.ds(p, 2), :, lanes].reshape(8 * cout, width)
            acc = dot(weights, rhs).astype(BF16)
            pairs = []
            for zy in range(4):
                even = acc[zy * 2 * cin : (zy * 2 + 1) * cin]
                odd = acc[(zy * 2 + 1) * cin : (zy * 2 + 2) * cin]
                for kk in range(group):
                    at = slice(kk * xs, (kk + 1) * xs)
                    pairs.append(jnp.concatenate([even[:, at], odd[:, at]], axis=1))
            joined = dot(jnp.concatenate(pairs, axis=0), join)
            for zy in range(4):
                for kk in range(group):
                    at = (zy * group + kk) * cin
                    for h in range(2):
                        y = 4 * (chunk * group + kk) + 2 * h + zy % 2
                        t_ref[zy // 2, pl.ds(y, cin, stride=ys), :] = joined[
                            at : at + cin, h * xs : (h + 1) * xs
                        ]
        for zp in range(2):
            out_ref[:, 2 * p + zp] = t_ref[zp].reshape(cin, ys, xs).astype(BF16)
        return carry

    lax.fori_loop(0, planes // 2, one, 0)


def call(kernel, outs, scratch=(), mib=24):
    return pl.pallas_call(
        kernel,
        out_shape=outs,
        scratch_shapes=scratch,
        compiler_params=pltpu.CompilerParams(vmem_limit_bytes=mib << 20),
    )


def shards(volume, kernel, cotangent):
    count = lax.axis_size("gz")
    everyone = count * lax.axis_size("vol")
    _, cin, planes, ys, xs = volume.shape
    _, cout, ozs, band, oxs = cotangent.shape
    slots = planes // 2
    blocks = ys // 4
    lanes = blocks * xs
    taps = jnp.transpose(kernel, (2, 3, 4, 1, 0)).reshape(27, cin, cout)

    grads = jnp.transpose(cotangent[0], (1, 0, 2, 3)).reshape(count, slots, cout, band * oxs)
    above = jnp.concatenate([grads[1:, :1], jnp.zeros_like(grads[:1, :1])], axis=0)
    packed = jnp.concatenate([grads, above], axis=1)
    recv = lax.all_to_all(packed, "gz", 0, 0, tiled=True)
    if band != 2:
        recv = recv.reshape(blocks, 2, slots + 1, cout, oxs)
        recv = jnp.transpose(recv, (0, 2, 3, 1, 4)).reshape(blocks, slots + 1, cout, xs)

    xx, send = call(
        forward_kernel,
        (
            jax.ShapeDtypeStruct((planes, 9 * cin, lanes), BF16),
            jax.ShapeDtypeStruct((blocks, slots + 1, cout, xs), BF16),
        ),
        (pltpu.VMEM((cin * ys, xs), F32), pltpu.VMEM((2, blocks * cin, 2 * xs), BF16)),
    )(volume[0], taps)
    if band != 2:
        send = send.reshape(blocks, slots + 1, cout, 2, oxs)
        send = jnp.transpose(send, (0, 3, 1, 2, 4)).reshape(count, slots + 1, cout, band * oxs)
        send = jnp.pad(send, ((0, 0), (0, 0), (0, 0), (0, xs - band * oxs)))
    send = send.reshape(count, (slots + 1) * cout, xs)
    unit = -(-(27 * cin // 2) // (16 * count)) * 16
    mix = call(
        weight_kernel,
        jax.ShapeDtypeStruct((count, (slots + 1) * cout + unit, xs), BF16),
    )(recv, xx, send)
    back = lax.all_to_all(mix, "gz", 0, 0, tiled=True)
    volumes = volume.shape[0] * lax.axis_size("vol")

    def add(back_ref, total_ref):
        sum_kernel(back_ref, total_ref, scale=1.0 / volumes)

    total = call(add, jax.ShapeDtypeStruct((everyone, unit, xs), BF16))(back)
    total = lax.all_to_all(total, ("vol", "gz"), 0, 0, tiled=True)
    back = back[:, : (slots + 1) * cout].reshape(count, slots + 1, cout, xs)
    carried = jnp.concatenate([jnp.zeros_like(back[:1, slots:]), back[:-1, slots:]], axis=0)
    first = (back[:, :1].astype(F32) + carried.astype(F32)).astype(BF16)
    whole = jnp.concatenate([first, back[:, 1:slots]], axis=1)
    whole = whole[..., : band * oxs].reshape(ozs, cout, band, oxs)
    features = jnp.transpose(whole, (1, 0, 2, 3))[None]

    volume_grad = call(
        input_kernel,
        jax.ShapeDtypeStruct((cin, planes, ys, xs), BF16),
        (
            pltpu.VMEM((slots + 1, 4 * cout, lanes), BF16),
            pltpu.VMEM((8 * cin, 8 * cout), BF16),
            pltpu.VMEM((2, cin * ys, xs), F32),
        ),
    )(recv, taps)[None]

    kernel_grad = call(final_kernel, jax.ShapeDtypeStruct((3, 9 * cin, cout), F32))(
        total.reshape(everyone // count, count, unit, xs)
    )
    kernel_grad = jnp.transpose(kernel_grad.reshape(3, 3, 3, cin, cout), (4, 3, 0, 1, 2))
    return (features, volume_grad, kernel_grad)


def solution(mesh):
    placed = (P("vol", None, "gz", None, None), P(), P("vol", None, None, "gz", None))
    return jax.shard_map(
        shards,
        mesh=mesh,
        in_specs=placed,
        out_specs=(P("vol", None, None, "gz", None), P("vol", None, "gz", None, None), P()),
        check_vma=False,
    )
```

```python
import jax
import jax.numpy as jnp
from jax import lax
from jax.experimental import pallas as pl
from jax.experimental.pallas import tpu as pltpu
from jax.sharding import PartitionSpec as P


F32 = jnp.float32
BF16 = jnp.bfloat16
TAP = {(0, 0): 1, (0, 1): 2, (1, 1): 0, (1, 0): None}


def dot(a, b):
    return lax.dot_general(a, b, (((1,), (0,)), ((), ())), preferred_element_type=F32)


def dot_t(a, b):
    return lax.dot_general(a, b, (((1,), (1,)), ((), ())), preferred_element_type=F32)


def iota(shape, dim):
    return lax.broadcasted_iota(jnp.int32, shape, dim)


def tap_matrix(x, swapped):
    shape = (2 * x, 3 * x)
    row, col = iota(shape, 0), iota(shape, 1)
    half_in, x_in = row // x, row % x
    tap, half_out, r = col // x, (col % x) // (x // 2), col % (x // 2)
    if swapped:
        half_out = 1 - half_out
    hit = (half_in == half_out) & (x_in == 2 * r + tap - 1)
    return jnp.where(hit, 1.0, 0.0).astype(BF16)


def join_matrix(x):
    shape = (2 * x, 2 * x)
    row, col = iota(shape, 0), iota(shape, 1)
    half_in, x_in = col // x, col % x
    parity, half_out, r = row // x, (row % x) // (x // 2), row % (x // 2)
    hit = (half_in == half_out) & (x_in == 2 * r + parity)
    return jnp.where(hit, 1.0, 0.0).astype(BF16)


def shift_matrix(x):
    shape = (2 * x, 3 * x)
    row, col = iota(shape, 0), iota(shape, 1)
    variant, lane = col // x + 1, col % x
    dq, dr = variant // 2, variant % 2
    hit = (row == lane + dq * (x // 2) + dr) & ((dr == 0) | (lane % (x // 2) != x // 2 - 1))
    return jnp.where(hit, 1.0, 0.0).astype(BF16)


def weight_block(k_ref, a, b, xp):
    if a is None or b is None:
        return jnp.zeros((k_ref.shape[1], 2 * k_ref.shape[2]), BF16)
    at = (a * 3 + b) * 3
    if xp == 0:
        one = k_ref[at + 1]
        return jnp.concatenate([one, jnp.zeros_like(one)], axis=1)
    return jnp.concatenate([k_ref[at + 2], k_ref[at]], axis=1)


def pack_kernel(cot_ref, vol_ref, packed_ref, plane_ref, c_ref, s_ref, sems):
    parts = c_ref.shape[0]
    copy = pltpu.make_async_copy(vol_ref.at[:, vol_ref.shape[1] - 1], plane_ref, sems.at[parts])
    copy.start()
    size = cot_ref.shape[0] // parts
    loads = [
        pltpu.make_async_copy(cot_ref.at[pl.ds(i * size, size)], c_ref.at[i], sems.at[i])
        for i in range(parts)
    ]
    for load in loads:
        load.start()
    count, slots, cout, xs = packed_ref.shape
    half = cot_ref.shape[1]
    own = cout // parts
    stride = size // own
    left = iota((own, xs), 1) < half
    for i in range(parts):
        loads[i].wait()
        s_ref[:, :half] = c_ref[i].astype(F32)
        for p in range(count * slots):
            low = s_ref[pl.ds(2 * p, own, stride=stride), :]
            high = s_ref[pl.ds(2 * p + 1, own, stride=stride), :]
            both = jnp.where(left, low, pltpu.roll(high, half, axis=1))
            packed_ref[p // slots, p % slots, pl.ds(i * own, own)] = both.astype(BF16)
    copy.wait()


def forward_kernel(vol_ref, halo_ref, k_ref, out_ref, mix_ref, xx_ref, t_ref, x_ref, sems):
    cin, planes, ys, xs = vol_ref.shape
    cout = k_ref.shape[2]
    blocks = ys // 4
    split = tap_matrix(xs, False)
    split_swapped = tap_matrix(xs, True)

    def expand(plane, z):
        t_ref[...] = plane.astype(F32).reshape(cin * ys, xs)
        for y in range(ys):
            k, h, yp = y // 4, (y // 2) % 2, y % 2
            rows = t_ref[pl.ds(y, cin, stride=ys), :]
            x_ref[yp, pl.ds(k * cin, cin), pl.ds(h * xs, xs)] = rows.astype(BF16)
        before = jnp.concatenate(
            [jnp.zeros((cin, xs), BF16), x_ref[1, : (blocks - 1) * cin, xs:]], axis=0
        )
        swapped = jnp.concatenate([x_ref[1, :, :xs], before], axis=1)
        for b, (pair, matrix) in enumerate(
            [(swapped, split_swapped), (x_ref[0], split), (x_ref[1], split)]
        ):
            out = dot(pair, matrix).astype(BF16)
            for k in range(blocks):
                for e in range(3):
                    xx_ref[z, pl.ds((b * 3 + e) * cin, cin), pl.ds(k * xs, xs)] = out[
                        k * cin : (k + 1) * cin, e * xs : (e + 1) * xs
                    ]

    def leave(z):
        return pltpu.make_async_copy(
            xx_ref.at[z, pl.ds(3 * cin, 6 * cin)], out_ref.at[z], sems.at[z]
        )

    def own(z, carry):
        expand(vol_ref[:, z], z + 1)
        leave(z + 1).start()
        return carry

    lax.fori_loop(0, planes, own, 0)
    expand(halo_ref[...], 0)
    leave(0).start()
    weights = jnp.transpose(k_ref[...].reshape(27 * cin, cout), (1, 0))
    group = 4
    width = group * xs

    def compute(chunk, carry):
        lanes = pl.ds(pl.multiple_of(chunk * width, width), width)
        for p in range(planes // 2):
            rhs = xx_ref[2 * p : 2 * p + 3, :, lanes].reshape(27 * cin, width)
            value = dot(weights, rhs).astype(BF16)
            for kk in range(group):
                mix_ref[chunk * group + kk, pl.ds(p * cout, cout), :] = value[
                    :, kk * xs : (kk + 1) * xs
                ]
        return carry

    lax.fori_loop(0, blocks // group, compute, 0)
    unit = mix_ref.shape[1] - planes // 2 * cout
    mix_ref[:, pl.ds(planes // 2 * cout, unit), :] = jnp.zeros((blocks, unit, xs), BF16)
    for z in range(planes + 1):
        leave(z).wait()


def weight_kernel(recv_ref, xx_ref, mix_in_ref, mix_ref, xx_vmem, part_vmem, sems):
    del mix_in_ref
    blocks, slots, cout, xs = recv_ref.shape
    planes, rows, _ = xx_ref.shape
    count, unit, _ = part_vmem.shape
    copies = [
        pltpu.make_async_copy(xx_ref.at[z], xx_vmem.at[z], sems.at[z]) for z in range(planes)
    ]
    third = rows // 2
    for z in range(0, planes, 2):
        copies[z].start()
    grads = [
        jnp.concatenate([recv_ref[k, p] for k in range(blocks)], axis=1) for p in range(slots)
    ]
    nexts = [
        jnp.concatenate([g[:, xs // 2 :], jnp.zeros((cout, xs // 2), BF16)], axis=1)
        for g in grads
    ]
    none = jnp.zeros_like(grads[0])

    def line(*pieces):
        return jnp.concatenate(pieces, axis=1)

    def stack(*pieces):
        return jnp.concatenate(pieces, axis=0)

    def taken(first, at):
        return line(*[xx_vmem[z, pl.ds(at, third)] for z in range(first, planes, 2)])

    for z in range(0, planes, 2):
        copies[z].wait()
    for z in range(1, planes, 2):
        copies[z].start()
    here = stack(line(none, *grads), line(*grads, none))
    after = stack(line(none, *nexts), line(*nexts, none))
    outer_two = dot_t(taken(0, third), stack(here, after))
    outer_one = dot_t(taken(0, 0), here)
    for z in range(1, planes, 2):
        copies[z].wait()
    inner_two = dot_t(taken(1, third), stack(line(*grads), line(*nexts)))
    inner_one = dot_t(taken(1, 0), line(*grads))
    part = stack(
        outer_two[:, : 2 * cout],
        outer_two[:, 2 * cout :],
        outer_one,
        inner_two,
        line(inner_one[: third // 2], inner_one[third // 2 :]),
        jnp.zeros((count * unit - 9 * third // 2, xs), F32),
    )
    part_vmem[...] = part.astype(BF16).reshape(count, unit, xs)
    out = pltpu.make_async_copy(
        part_vmem, mix_ref.at[:, pl.ds(slots * cout, unit)], sems.at[planes]
    )
    out.start()
    out.wait()


def sum_kernel(back_ref, total_ref, *, scale):
    count, rows, _ = back_ref.shape
    everyone, unit, _ = total_ref.shape
    total = None
    for k in range(count):
        piece = back_ref[k, pl.ds(rows - unit, unit), :].astype(F32)
        total = piece if total is None else total + piece
    total = (total * scale).astype(BF16)
    for k in range(everyone):
        total_ref[k] = total


def final_kernel(total_ref, out_ref):
    _, rows, cout = out_ref.shape
    volumes, count, unit, xs = total_ref.shape
    total = total_ref[0].astype(F32)
    for v in range(1, volumes):
        total = total + total_ref[v].astype(F32)
    total = total.reshape(count * unit, xs)
    third = rows // 3
    for at, b in enumerate((2, 0, 1)):
        piece = total[at * third : (at + 1) * third]
        out_ref[2, pl.ds(b * third, third), :] = piece[:, :cout]
        out_ref[0, pl.ds(b * third, third), :] = piece[:, cout:]
    piece = total[3 * third : 4 * third]
    out_ref[1, pl.ds(2 * third, third), :] = piece[:, :cout]
    out_ref[1, pl.ds(0, third), :] = piece[:, cout:]
    piece = total[4 * third : 4 * third + third // 2]
    out_ref[1, pl.ds(third, third // 2), :] = piece[:, :cout]
    out_ref[1, pl.ds(third + third // 2, third // 2), :] = piece[:, cout:]


def input_kernel(recv_ref, halo_ref, k_ref, out_ref, gg_ref, w_ref, t_ref):
    cin, planes, ys, xs = out_ref.shape
    blocks, slots, cout, _ = recv_ref.shape
    shifts = shift_matrix(xs)

    def shifted(p, here):
        after = jnp.concatenate([here[cout:], jnp.zeros((cout, xs), BF16)], axis=0)
        out = dot(jnp.concatenate([here, after], axis=1), shifts).astype(BF16)
        for k in range(blocks):
            lanes = pl.ds(k * xs, xs)
            rows = slice(k * cout, (k + 1) * cout)
            gg_ref[p, pl.ds(0, cout), lanes] = here[rows]
            for v in range(1, 4):
                gg_ref[p, pl.ds(v * cout, cout), lanes] = out[rows, (v - 1) * xs : v * xs]

    for p in range(slots):
        shifted(p, recv_ref[:, p].reshape(blocks * cout, xs))
    shifted(slots, halo_ref[...].reshape(blocks * cout, xs))
    for zp in range(2):
        for yp in range(2):
            for xp in range(2):
                for dp in range(2):
                    for dq in range(2):
                        w_ref[
                            pl.ds(((zp * 2 + yp) * 2 + xp) * cin, cin),
                            pl.ds((dp * 2 + dq) * 2 * cout, 2 * cout),
                        ] = weight_block(k_ref, TAP[dp, zp], TAP[dq, yp], xp)
    join = join_matrix(xs)
    weights = w_ref[...]
    group = 4
    width = group * xs

    def one(p, carry):
        for chunk in range(blocks // group):
            lanes = pl.ds(chunk * width, width)
            rhs = gg_ref[pl.ds(p, 2), :, lanes].reshape(8 * cout, width)
            acc = dot(weights, rhs).astype(BF16)
            pairs = []
            for zy in range(4):
                even = acc[zy * 2 * cin : (zy * 2 + 1) * cin]
                odd = acc[(zy * 2 + 1) * cin : (zy * 2 + 2) * cin]
                for kk in range(group):
                    at = slice(kk * xs, (kk + 1) * xs)
                    pairs.append(jnp.concatenate([even[:, at], odd[:, at]], axis=1))
            joined = dot(jnp.concatenate(pairs, axis=0), join)
            for zy in range(4):
                for kk in range(group):
                    at = (zy * group + kk) * cin
                    for h in range(2):
                        y = 4 * (chunk * group + kk) + 2 * h + zy % 2
                        t_ref[zy // 2, pl.ds(y, cin, stride=ys), :] = joined[
                            at : at + cin, h * xs : (h + 1) * xs
                        ]
        for zp in range(2):
            out_ref[:, 2 * p + zp] = t_ref[zp].reshape(cin, ys, xs).astype(BF16)
        return carry

    lax.fori_loop(0, planes // 2, one, 0)


def call(kernel, outs, scratch=(), mib=24, **kwargs):
    return pl.pallas_call(
        kernel,
        out_shape=outs,
        scratch_shapes=scratch,
        compiler_params=pltpu.CompilerParams(vmem_limit_bytes=mib << 20),
        **kwargs,
    )


def stay(value):
    return pltpu.with_memory_space_constraint(value, pltpu.HBM)


HBM = pl.BlockSpec(memory_space=pltpu.HBM)
VMEM = pl.BlockSpec(memory_space=pltpu.VMEM)


def shards(volume, kernel, cotangent):
    count = lax.axis_size("gz")
    everyone = count * lax.axis_size("vol")
    _, cin, planes, ys, xs = volume.shape
    _, cout, ozs, band, oxs = cotangent.shape
    slots = planes // 2
    blocks = ys // 4
    lanes = blocks * xs
    unit = -(-(27 * cin // 2) // (16 * blocks)) * 16
    taps = jnp.transpose(kernel, (2, 3, 4, 1, 0)).reshape(27, cin, cout)

    if band == 2:
        packed, plane = call(
            pack_kernel,
            (
                jax.ShapeDtypeStruct((count, slots, cout, xs), BF16),
                jax.ShapeDtypeStruct((cin, ys, xs), BF16),
            ),
            (
                pltpu.VMEM((4, cout * ozs * band // 4, oxs), BF16),
                pltpu.VMEM((cout * ozs * band // 4, xs), F32),
                pltpu.SemaphoreType.DMA((5,)),
            ),
            in_specs=(HBM, HBM),
            out_specs=(VMEM, VMEM),
        )(stay(cotangent.reshape(cout * ozs * band, oxs)), stay(volume[0]))
    else:
        packed = jnp.transpose(cotangent[0], (1, 0, 2, 3)).reshape(count, slots, cout, band * oxs)
        plane = volume[0, :, planes - 1]
    under = lax.ppermute(plane, "gz", [(i, i + 1) for i in range(count - 1)])
    recv = lax.all_to_all(packed, "gz", 0, 0, tiled=True)
    if band != 2:
        recv = recv.reshape(blocks, 2 // band, slots, cout, band, oxs)
        recv = jnp.transpose(recv, (0, 2, 3, 1, 4, 5)).reshape(blocks, slots, cout, xs)
    above = lax.ppermute(recv[:, 0], "gz", [(i + 1, i) for i in range(count - 1)])

    xx, mix = call(
        forward_kernel,
        (
            pltpu.HBM((planes + 1, 6 * cin, lanes), BF16),
            pltpu.HBM((blocks, slots * cout + unit, xs), BF16),
        ),
        (
            pltpu.VMEM((planes + 1, 9 * cin, lanes), BF16),
            pltpu.VMEM((cin * ys, xs), F32),
            pltpu.VMEM((2, blocks * cin, 2 * xs), BF16),
            pltpu.SemaphoreType.DMA((planes + 1,)),
        ),
        in_specs=(VMEM, VMEM, VMEM),
        out_specs=(HBM, VMEM),
    )(volume[0], under, taps)
    mix = call(
        weight_kernel,
        pltpu.HBM(mix.shape, BF16),
        (
            pltpu.VMEM(xx.shape, BF16),
            pltpu.VMEM((blocks, unit, xs), BF16),
            pltpu.SemaphoreType.DMA((planes + 2,)),
        ),
        in_specs=(VMEM, HBM, HBM),
        out_specs=HBM,
        input_output_aliases={2: 0},
    )(recv, stay(xx), stay(mix))
    if band != 2:
        send = mix[:, : slots * cout].reshape(blocks, slots * cout, 2 // band, band * oxs)
        send = jnp.transpose(send, (0, 2, 1, 3)).reshape(count, slots * cout, band * oxs)
        send = jnp.pad(send, ((0, 0), (0, 0), (0, xs - band * oxs)))
        terms = mix[:, slots * cout :].reshape(count, blocks * unit // count, xs)
        mix = jnp.concatenate([send, terms], axis=1)
        unit = terms.shape[1]
    back = lax.all_to_all(mix, "gz", 0, 0, tiled=True)
    volumes = volume.shape[0] * lax.axis_size("vol")

    def add(back_ref, total_ref):
        sum_kernel(back_ref, total_ref, scale=1.0 / volumes)

    total = call(add, jax.ShapeDtypeStruct((everyone, unit, xs), BF16))(back)
    total = lax.all_to_all(total, ("vol", "gz"), 0, 0, tiled=True)
    features = back[:, : slots * cout, : band * oxs].reshape(ozs, cout, band, oxs)
    features = jnp.transpose(features, (1, 0, 2, 3))[None]

    volume_grad = call(
        input_kernel,
        jax.ShapeDtypeStruct((cin, planes, ys, xs), BF16),
        (
            pltpu.VMEM((slots + 1, 4 * cout, lanes), BF16),
            pltpu.VMEM((8 * cin, 8 * cout), BF16),
            pltpu.VMEM((2, cin * ys, xs), F32),
        ),
    )(recv, above, taps)[None]

    kernel_grad = call(final_kernel, jax.ShapeDtypeStruct((3, 9 * cin, cout), F32))(
        total.reshape(everyone // count, count, unit, xs)
    )
    kernel_grad = jnp.transpose(kernel_grad.reshape(3, 3, 3, cin, cout), (4, 3, 0, 1, 2))
    return (features, volume_grad, kernel_grad)


def solution(mesh):
    placed = (P("vol", None, "gz", None, None), P(), P("vol", None, None, "gz", None))
    return jax.shard_map(
        shards,
        mesh=mesh,
        in_specs=placed,
        out_specs=(P("vol", None, None, "gz", None), P("vol", None, "gz", None, None), P()),
        check_vma=False,
    )
```

```python
import jax
import jax.numpy as jnp
from jax import lax
from jax.experimental import pallas as pl
from jax.experimental.pallas import tpu as pltpu
from jax.sharding import PartitionSpec as P


F32 = jnp.float32
BF16 = jnp.bfloat16
TAP = {(0, 0): 1, (0, 1): 2, (1, 1): 0, (1, 0): None}


def dot(a, b):
    return lax.dot_general(a, b, (((1,), (0,)), ((), ())), preferred_element_type=F32)


def dot_t(a, b):
    return lax.dot_general(a, b, (((1,), (1,)), ((), ())), preferred_element_type=F32)


def iota(shape, dim):
    return lax.broadcasted_iota(jnp.int32, shape, dim)


def tap_matrix(x, swapped):
    shape = (2 * x, 3 * x)
    row, col = iota(shape, 0), iota(shape, 1)
    half_in, x_in = row // x, row % x
    tap, half_out, r = col // x, (col % x) // (x // 2), col % (x // 2)
    if swapped:
        half_out = 1 - half_out
    hit = (half_in == half_out) & (x_in == 2 * r + tap - 1)
    return jnp.where(hit, 1.0, 0.0).astype(BF16)


def join_matrix(x):
    shape = (2 * x, 2 * x)
    row, col = iota(shape, 0), iota(shape, 1)
    half_in, x_in = col // x, col % x
    parity, half_out, r = row // x, (row % x) // (x // 2), row % (x // 2)
    hit = (half_in == half_out) & (x_in == 2 * r + parity)
    return jnp.where(hit, 1.0, 0.0).astype(BF16)


def shift_matrix(x):
    shape = (2 * x, 3 * x)
    row, col = iota(shape, 0), iota(shape, 1)
    variant, lane = col // x + 1, col % x
    dq, dr = variant // 2, variant % 2
    hit = (row == lane + dq * (x // 2) + dr) & ((dr == 0) | (lane % (x // 2) != x // 2 - 1))
    return jnp.where(hit, 1.0, 0.0).astype(BF16)


def weight_block(k_ref, a, b, xp):
    if a is None or b is None:
        return jnp.zeros((k_ref.shape[1], 2 * k_ref.shape[2]), BF16)
    at = (a * 3 + b) * 3
    if xp == 0:
        one = k_ref[at + 1]
        return jnp.concatenate([one, jnp.zeros_like(one)], axis=1)
    return jnp.concatenate([k_ref[at + 2], k_ref[at]], axis=1)


def pack_kernel(cot_ref, vol_ref, packed_ref, plane_ref, c_ref, s_ref, sems):
    parts = c_ref.shape[0]
    copy = pltpu.make_async_copy(vol_ref.at[:, vol_ref.shape[1] - 1], plane_ref, sems.at[parts])
    copy.start()
    size = cot_ref.shape[0] // parts
    loads = [
        pltpu.make_async_copy(cot_ref.at[pl.ds(i * size, size)], c_ref.at[i], sems.at[i])
        for i in range(parts)
    ]
    for load in loads:
        load.start()
    count, slots, cout, xs = packed_ref.shape
    half = cot_ref.shape[1]
    own = cout // parts
    stride = size // own
    left = iota((own, xs), 1) < half
    for i in range(parts):
        loads[i].wait()
        s_ref[:, :half] = c_ref[i].astype(F32)
        for p in range(count * slots):
            low = s_ref[pl.ds(2 * p, own, stride=stride), :]
            high = s_ref[pl.ds(2 * p + 1, own, stride=stride), :]
            both = jnp.where(left, low, pltpu.roll(high, half, axis=1))
            packed_ref[p // slots, p % slots, pl.ds(i * own, own)] = both.astype(BF16)
    copy.wait()


def forward_kernel(vol_ref, halo_ref, k_ref, out_ref, mix_ref, xx_ref, t_ref, x_ref, sems):
    cin, planes, ys, xs = vol_ref.shape
    cout = k_ref.shape[2]
    blocks = ys // 4
    split = tap_matrix(xs, False)
    split_swapped = tap_matrix(xs, True)

    def expand(plane, z):
        t_ref[...] = plane.astype(F32).reshape(cin * ys, xs)
        for y in range(ys):
            k, h, yp = y // 4, (y // 2) % 2, y % 2
            rows = t_ref[pl.ds(y, cin, stride=ys), :]
            x_ref[yp, pl.ds(k * cin, cin), pl.ds(h * xs, xs)] = rows.astype(BF16)
        before = jnp.concatenate(
            [jnp.zeros((cin, xs), BF16), x_ref[1, : (blocks - 1) * cin, xs:]], axis=0
        )
        swapped = jnp.concatenate([x_ref[1, :, :xs], before], axis=1)
        for b, (pair, matrix) in enumerate(
            [(swapped, split_swapped), (x_ref[0], split), (x_ref[1], split)]
        ):
            out = dot(pair, matrix).astype(BF16)
            for k in range(blocks):
                for e in range(3):
                    xx_ref[z, pl.ds((b * 3 + e) * cin, cin), pl.ds(k * xs, xs)] = out[
                        k * cin : (k + 1) * cin, e * xs : (e + 1) * xs
                    ]

    def leave(z):
        return pltpu.make_async_copy(
            xx_ref.at[z, pl.ds(3 * cin, 6 * cin)], out_ref.at[z], sems.at[z]
        )

    def own(z, carry):
        expand(vol_ref[:, z], z + 1)
        leave(z + 1).start()
        return carry

    lax.fori_loop(0, planes, own, 0)
    expand(halo_ref[...], 0)
    leave(0).start()
    weights = jnp.transpose(k_ref[...].reshape(27 * cin, cout), (1, 0))
    group = 4
    width = group * xs

    def compute(chunk, carry):
        lanes = pl.ds(pl.multiple_of(chunk * width, width), width)
        for p in range(planes // 2):
            rhs = xx_ref[2 * p : 2 * p + 3, :, lanes].reshape(27 * cin, width)
            value = dot(weights, rhs).astype(BF16)
            for kk in range(group):
                mix_ref[chunk * group + kk, pl.ds(p * cout, cout), :] = value[
                    :, kk * xs : (kk + 1) * xs
                ]
        return carry

    lax.fori_loop(0, blocks // group, compute, 0)
    unit = mix_ref.shape[1] - planes // 2 * cout
    mix_ref[:, pl.ds(planes // 2 * cout, unit), :] = jnp.zeros((blocks, unit, xs), BF16)
    for z in range(planes + 1):
        leave(z).wait()


def weight_kernel(recv_ref, xx_ref, mix_in_ref, mix_ref, part_vmem, sem):
    del mix_in_ref
    blocks, slots, cout, xs = recv_ref.shape
    planes, rows, _ = xx_ref.shape
    count, unit, _ = part_vmem.shape
    third = rows // 2
    grads = [
        jnp.concatenate([recv_ref[k, p] for k in range(blocks)], axis=1) for p in range(slots)
    ]
    nexts = [
        jnp.concatenate([g[:, xs // 2 :], jnp.zeros((cout, xs // 2), BF16)], axis=1)
        for g in grads
    ]
    none = jnp.zeros_like(grads[0])

    def line(*pieces):
        return jnp.concatenate(pieces, axis=1)

    def stack(*pieces):
        return jnp.concatenate(pieces, axis=0)

    def taken(first, at):
        return line(*[xx_ref[z, pl.ds(at, third)] for z in range(first, planes, 2)])

    here = stack(line(none, *grads), line(*grads, none))
    after = stack(line(none, *nexts), line(*nexts, none))
    outer_two = dot_t(taken(0, third), stack(here, after))
    outer_one = dot_t(taken(0, 0), here)
    inner_two = dot_t(taken(1, third), stack(line(*grads), line(*nexts)))
    inner_one = dot_t(taken(1, 0), line(*grads))
    part = stack(
        outer_two[:, : 2 * cout],
        outer_two[:, 2 * cout :],
        outer_one,
        inner_two,
        line(inner_one[: third // 2], inner_one[third // 2 :]),
        jnp.zeros((count * unit - 9 * third // 2, xs), F32),
    )
    part_vmem[...] = part.astype(BF16).reshape(count, unit, xs)
    out = pltpu.make_async_copy(
        part_vmem, mix_ref.at[:, pl.ds(slots * cout, unit)], sem
    )
    out.start()
    out.wait()


def sum_kernel(back_ref, total_ref, *, scale):
    count, rows, _ = back_ref.shape
    everyone, unit, _ = total_ref.shape
    total = None
    for k in range(count):
        piece = back_ref[k, pl.ds(rows - unit, unit), :].astype(F32)
        total = piece if total is None else total + piece
    total = (total * scale).astype(BF16)
    for k in range(everyone):
        total_ref[k] = total


def final_kernel(total_ref, out_ref):
    _, rows, cout = out_ref.shape
    volumes, count, unit, xs = total_ref.shape
    total = total_ref[0].astype(F32)
    for v in range(1, volumes):
        total = total + total_ref[v].astype(F32)
    total = total.reshape(count * unit, xs)
    third = rows // 3
    for at, b in enumerate((2, 0, 1)):
        piece = total[at * third : (at + 1) * third]
        out_ref[2, pl.ds(b * third, third), :] = piece[:, :cout]
        out_ref[0, pl.ds(b * third, third), :] = piece[:, cout:]
    piece = total[3 * third : 4 * third]
    out_ref[1, pl.ds(2 * third, third), :] = piece[:, :cout]
    out_ref[1, pl.ds(0, third), :] = piece[:, cout:]
    piece = total[4 * third : 4 * third + third // 2]
    out_ref[1, pl.ds(third, third // 2), :] = piece[:, :cout]
    out_ref[1, pl.ds(third + third // 2, third // 2), :] = piece[:, cout:]


def input_kernel(recv_ref, halo_ref, k_ref, out_ref, gg_ref, w_ref, t_ref):
    cin, planes, ys, xs = out_ref.shape
    blocks, slots, cout, _ = recv_ref.shape
    shifts = shift_matrix(xs)

    def shifted(p, here):
        after = jnp.concatenate([here[cout:], jnp.zeros((cout, xs), BF16)], axis=0)
        out = dot(jnp.concatenate([here, after], axis=1), shifts).astype(BF16)
        for k in range(blocks):
            lanes = pl.ds(k * xs, xs)
            rows = slice(k * cout, (k + 1) * cout)
            gg_ref[p, pl.ds(0, cout), lanes] = here[rows]
            for v in range(1, 4):
                gg_ref[p, pl.ds(v * cout, cout), lanes] = out[rows, (v - 1) * xs : v * xs]

    for p in range(slots):
        shifted(p, recv_ref[:, p].reshape(blocks * cout, xs))
    shifted(slots, halo_ref[...].reshape(blocks * cout, xs))
    for zp in range(2):
        for yp in range(2):
            for xp in range(2):
                for dp in range(2):
                    for dq in range(2):
                        w_ref[
                            pl.ds(((zp * 2 + yp) * 2 + xp) * cin, cin),
                            pl.ds((dp * 2 + dq) * 2 * cout, 2 * cout),
                        ] = weight_block(k_ref, TAP[dp, zp], TAP[dq, yp], xp)
    join = join_matrix(xs)
    weights = w_ref[...]
    group = 4
    width = group * xs

    def one(p, carry):
        for chunk in range(blocks // group):
            lanes = pl.ds(chunk * width, width)
            rhs = gg_ref[pl.ds(p, 2), :, lanes].reshape(8 * cout, width)
            acc = dot(weights, rhs).astype(BF16)
            pairs = []
            for zy in range(4):
                even = acc[zy * 2 * cin : (zy * 2 + 1) * cin]
                odd = acc[(zy * 2 + 1) * cin : (zy * 2 + 2) * cin]
                for kk in range(group):
                    at = slice(kk * xs, (kk + 1) * xs)
                    pairs.append(jnp.concatenate([even[:, at], odd[:, at]], axis=1))
            joined = dot(jnp.concatenate(pairs, axis=0), join)
            for zy in range(4):
                for kk in range(group):
                    at = (zy * group + kk) * cin
                    for h in range(2):
                        y = 4 * (chunk * group + kk) + 2 * h + zy % 2
                        t_ref[zy // 2, pl.ds(y, cin, stride=ys), :] = joined[
                            at : at + cin, h * xs : (h + 1) * xs
                        ]
        for zp in range(2):
            out_ref[:, 2 * p + zp] = t_ref[zp].reshape(cin, ys, xs).astype(BF16)
        return carry

    lax.fori_loop(0, planes // 2, one, 0)


def call(kernel, outs, scratch=(), mib=24, **kwargs):
    return pl.pallas_call(
        kernel,
        out_shape=outs,
        scratch_shapes=scratch,
        compiler_params=pltpu.CompilerParams(vmem_limit_bytes=mib << 20),
        **kwargs,
    )


def stay(value):
    return pltpu.with_memory_space_constraint(value, pltpu.HBM)


HBM = pl.BlockSpec(memory_space=pltpu.HBM)
VMEM = pl.BlockSpec(memory_space=pltpu.VMEM)


def shards(volume, kernel, cotangent):
    count = lax.axis_size("gz")
    everyone = count * lax.axis_size("vol")
    _, cin, planes, ys, xs = volume.shape
    _, cout, ozs, band, oxs = cotangent.shape
    slots = planes // 2
    blocks = ys // 4
    lanes = blocks * xs
    unit = -(-(27 * cin // 2) // (16 * blocks)) * 16
    taps = jnp.transpose(kernel, (2, 3, 4, 1, 0)).reshape(27, cin, cout)

    if band == 2:
        packed, plane = call(
            pack_kernel,
            (
                jax.ShapeDtypeStruct((count, slots, cout, xs), BF16),
                jax.ShapeDtypeStruct((cin, ys, xs), BF16),
            ),
            (
                pltpu.VMEM((4, cout * ozs * band // 4, oxs), BF16),
                pltpu.VMEM((cout * ozs * band // 4, xs), F32),
                pltpu.SemaphoreType.DMA((5,)),
            ),
            in_specs=(HBM, HBM),
            out_specs=(VMEM, VMEM),
        )(stay(cotangent.reshape(cout * ozs * band, oxs)), stay(volume[0]))
    else:
        packed = jnp.transpose(cotangent[0], (1, 0, 2, 3)).reshape(count, slots, cout, band * oxs)
        plane = volume[0, :, planes - 1]
    under = lax.ppermute(plane, "gz", [(i, i + 1) for i in range(count - 1)])
    recv = lax.all_to_all(packed, "gz", 0, 0, tiled=True)
    if band != 2:
        recv = recv.reshape(blocks, 2 // band, slots, cout, band, oxs)
        recv = jnp.transpose(recv, (0, 2, 3, 1, 4, 5)).reshape(blocks, slots, cout, xs)
    above = lax.ppermute(recv[:, 0], "gz", [(i + 1, i) for i in range(count - 1)])

    xx, mix = call(
        forward_kernel,
        (
            pltpu.HBM((planes + 1, 6 * cin, lanes), BF16),
            pltpu.HBM((blocks, slots * cout + unit, xs), BF16),
        ),
        (
            pltpu.VMEM((planes + 1, 9 * cin, lanes), BF16),
            pltpu.VMEM((cin * ys, xs), F32),
            pltpu.VMEM((2, blocks * cin, 2 * xs), BF16),
            pltpu.SemaphoreType.DMA((planes + 1,)),
        ),
        in_specs=(VMEM, VMEM, VMEM),
        out_specs=(HBM, VMEM),
    )(volume[0], under, taps)
    mix = call(
        weight_kernel,
        pltpu.HBM(mix.shape, BF16),
        (
            pltpu.VMEM((blocks, unit, xs), BF16),
            pltpu.SemaphoreType.DMA,
        ),
        in_specs=(VMEM, VMEM, HBM),
        out_specs=HBM,
        input_output_aliases={2: 0},
    )(recv, xx, stay(mix))
    if band != 2:
        send = mix[:, : slots * cout].reshape(blocks, slots * cout, 2 // band, band * oxs)
        send = jnp.transpose(send, (0, 2, 1, 3)).reshape(count, slots * cout, band * oxs)
        send = jnp.pad(send, ((0, 0), (0, 0), (0, xs - band * oxs)))
        terms = mix[:, slots * cout :].reshape(count, blocks * unit // count, xs)
        mix = jnp.concatenate([send, terms], axis=1)
        unit = terms.shape[1]
    back = lax.all_to_all(mix, "gz", 0, 0, tiled=True)
    volumes = volume.shape[0] * lax.axis_size("vol")

    def add(back_ref, total_ref):
        sum_kernel(back_ref, total_ref, scale=1.0 / volumes)

    total = call(add, jax.ShapeDtypeStruct((everyone, unit, xs), BF16))(back)
    total = lax.all_to_all(total, ("vol", "gz"), 0, 0, tiled=True)
    features = back[:, : slots * cout, : band * oxs].reshape(ozs, cout, band, oxs)
    features = jnp.transpose(features, (1, 0, 2, 3))[None]

    volume_grad = call(
        input_kernel,
        jax.ShapeDtypeStruct((cin, planes, ys, xs), BF16),
        (
            pltpu.VMEM((slots + 1, 4 * cout, lanes), BF16),
            pltpu.VMEM((8 * cin, 8 * cout), BF16),
            pltpu.VMEM((2, cin * ys, xs), F32),
        ),
    )(recv, above, taps)[None]

    kernel_grad = call(final_kernel, jax.ShapeDtypeStruct((3, 9 * cin, cout), F32))(
        total.reshape(everyone // count, count, unit, xs)
    )
    kernel_grad = jnp.transpose(kernel_grad.reshape(3, 3, 3, cin, cout), (4, 3, 0, 1, 2))
    return (features, volume_grad, kernel_grad)


def solution(mesh):
    placed = (P("vol", None, "gz", None, None), P(), P("vol", None, None, "gz", None))
    return jax.shard_map(
        shards,
        mesh=mesh,
        in_specs=placed,
        out_specs=(P("vol", None, None, "gz", None), P("vol", None, "gz", None, None), P()),
        check_vma=False,
    )
```

```python
import jax
import jax.numpy as jnp
from jax import lax
from jax.experimental import pallas as pl
from jax.experimental.pallas import tpu as pltpu
from jax.sharding import PartitionSpec as P


F32 = jnp.float32
BF16 = jnp.bfloat16
TAP = {(0, 0): 1, (0, 1): 2, (1, 1): 0, (1, 0): None}


def dot(a, b):
    return lax.dot_general(a, b, (((1,), (0,)), ((), ())), preferred_element_type=F32)


def dot_t(a, b):
    return lax.dot_general(a, b, (((1,), (1,)), ((), ())), preferred_element_type=F32)


def iota(shape, dim):
    return lax.broadcasted_iota(jnp.int32, shape, dim)


def tap_matrix(x, swapped):
    shape = (2 * x, 3 * x)
    row, col = iota(shape, 0), iota(shape, 1)
    half_in, x_in = row // x, row % x
    tap, half_out, r = col // x, (col % x) // (x // 2), col % (x // 2)
    if swapped:
        half_out = 1 - half_out
    hit = (half_in == half_out) & (x_in == 2 * r + tap - 1)
    return jnp.where(hit, 1.0, 0.0).astype(BF16)


def join_matrix(x):
    shape = (2 * x, 2 * x)
    row, col = iota(shape, 0), iota(shape, 1)
    half_in, x_in = col // x, col % x
    parity, half_out, r = row // x, (row % x) // (x // 2), row % (x // 2)
    hit = (half_in == half_out) & (x_in == 2 * r + parity)
    return jnp.where(hit, 1.0, 0.0).astype(BF16)


def shift_matrix(x):
    shape = (2 * x, 3 * x)
    row, col = iota(shape, 0), iota(shape, 1)
    variant, lane = col // x + 1, col % x
    dq, dr = variant // 2, variant % 2
    hit = (row == lane + dq * (x // 2) + dr) & ((dr == 0) | (lane % (x // 2) != x // 2 - 1))
    return jnp.where(hit, 1.0, 0.0).astype(BF16)


def weight_block(k_ref, a, b, xp):
    if a is None or b is None:
        return jnp.zeros((k_ref.shape[1], 2 * k_ref.shape[2]), BF16)
    at = (a * 3 + b) * 3
    if xp == 0:
        one = k_ref[at + 1]
        return jnp.concatenate([one, jnp.zeros_like(one)], axis=1)
    return jnp.concatenate([k_ref[at + 2], k_ref[at]], axis=1)


def pack_kernel(cot_ref, vol_ref, packed_ref, plane_ref, c_ref, s_ref, sems):
    parts = c_ref.shape[0]
    copy = pltpu.make_async_copy(vol_ref.at[:, vol_ref.shape[1] - 1], plane_ref, sems.at[parts])
    copy.start()
    size = cot_ref.shape[0] // parts
    loads = [
        pltpu.make_async_copy(cot_ref.at[pl.ds(i * size, size)], c_ref.at[i], sems.at[i])
        for i in range(parts)
    ]
    for load in loads:
        load.start()
    count, slots, cout, xs = packed_ref.shape
    half = cot_ref.shape[1]
    own = cout // parts
    stride = size // own
    left = iota((own, xs), 1) < half
    for i in range(parts):
        loads[i].wait()
        s_ref[:, :half] = c_ref[i].astype(F32)
        for p in range(count * slots):
            low = s_ref[pl.ds(2 * p, own, stride=stride), :]
            high = s_ref[pl.ds(2 * p + 1, own, stride=stride), :]
            both = jnp.where(left, low, pltpu.roll(high, half, axis=1))
            packed_ref[p // slots, p % slots, pl.ds(i * own, own)] = both.astype(BF16)
    copy.wait()


def forward_kernel(vol_ref, halo_ref, k_ref, out_ref, mix_ref, xx_ref, t_ref, x_ref, sems):
    cin, planes, ys, xs = vol_ref.shape
    cout = k_ref.shape[2]
    blocks = ys // 4
    split = tap_matrix(xs, False)
    split_swapped = tap_matrix(xs, True)

    def expand(plane, z):
        t_ref[...] = plane.astype(F32).reshape(cin * ys, xs)
        for y in range(ys):
            k, h, yp = y // 4, (y // 2) % 2, y % 2
            rows = t_ref[pl.ds(y, cin, stride=ys), :]
            x_ref[yp, pl.ds(k * cin, cin), pl.ds(h * xs, xs)] = rows.astype(BF16)
        before = jnp.concatenate(
            [jnp.zeros((cin, xs), BF16), x_ref[1, : (blocks - 1) * cin, xs:]], axis=0
        )
        swapped = jnp.concatenate([x_ref[1, :, :xs], before], axis=1)
        for b, (pair, matrix) in enumerate(
            [(swapped, split_swapped), (x_ref[0], split), (x_ref[1], split)]
        ):
            out = dot(pair, matrix).astype(BF16)
            for k in range(blocks):
                for e in range(3):
                    xx_ref[z, pl.ds((b * 3 + e) * cin, cin), pl.ds(k * xs, xs)] = out[
                        k * cin : (k + 1) * cin, e * xs : (e + 1) * xs
                    ]

    def leave(z):
        return pltpu.make_async_copy(
            xx_ref.at[z, pl.ds(3 * cin, 6 * cin)], out_ref.at[z], sems.at[z]
        )

    def own(z, carry):
        expand(vol_ref[:, z], z + 1)
        leave(z + 1).start()
        return carry

    lax.fori_loop(0, planes, own, 0)
    expand(halo_ref[...], 0)
    leave(0).start()
    weights = jnp.transpose(k_ref[...].reshape(27 * cin, cout), (1, 0))
    group = 4
    width = group * xs

    def compute(chunk, carry):
        lanes = pl.ds(pl.multiple_of(chunk * width, width), width)
        for p in range(planes // 2):
            rhs = xx_ref[2 * p : 2 * p + 3, :, lanes].reshape(27 * cin, width)
            value = dot(weights, rhs).astype(BF16)
            for kk in range(group):
                mix_ref[chunk * group + kk, pl.ds(p * cout, cout), :] = value[
                    :, kk * xs : (kk + 1) * xs
                ]
        return carry

    lax.fori_loop(0, blocks // group, compute, 0)
    unit = mix_ref.shape[1] - planes // 2 * cout
    mix_ref[:, pl.ds(planes // 2 * cout, unit), :] = jnp.zeros((blocks, unit, xs), BF16)
    for z in range(planes + 1):
        leave(z).wait()


def weight_kernel(recv_ref, xx_ref, mix_in_ref, mix_ref, part_vmem, sem):
    del mix_in_ref
    blocks, slots, cout, xs = recv_ref.shape
    planes, rows, _ = xx_ref.shape
    count, unit, _ = part_vmem.shape
    third = rows // 2
    grads = [
        jnp.concatenate([recv_ref[k, p] for k in range(blocks)], axis=1) for p in range(slots)
    ]
    nexts = [
        jnp.concatenate([g[:, xs // 2 :], jnp.zeros((cout, xs // 2), BF16)], axis=1)
        for g in grads
    ]
    none = jnp.zeros_like(grads[0])

    def line(*pieces):
        return jnp.concatenate(pieces, axis=1)

    def stack(*pieces):
        return jnp.concatenate(pieces, axis=0)

    def taken(first, at):
        return line(*[xx_ref[z, pl.ds(at, third)] for z in range(first, planes, 2)])

    here = stack(line(none, *grads), line(*grads, none))
    after = stack(line(none, *nexts), line(*nexts, none))
    outer_two = dot_t(taken(0, third), stack(here, after))
    outer_one = dot_t(taken(0, 0), here)
    inner_two = dot_t(taken(1, third), stack(line(*grads), line(*nexts)))
    inner_one = dot_t(taken(1, 0), line(*grads))
    part = stack(
        outer_two[:, : 2 * cout],
        outer_two[:, 2 * cout :],
        outer_one,
        inner_two,
        line(inner_one[: third // 2], inner_one[third // 2 :]),
        jnp.zeros((count * unit - 9 * third // 2, xs), F32),
    )
    part_vmem[...] = part.astype(BF16).reshape(count, unit, xs)
    out = pltpu.make_async_copy(
        part_vmem, mix_ref.at[:, pl.ds(slots * cout, unit)], sem
    )
    out.start()
    out.wait()


def sum_kernel(back_ref, total_ref, *, scale):
    count, rows, _ = back_ref.shape
    everyone, unit, _ = total_ref.shape
    total = None
    for k in range(count):
        piece = back_ref[k, pl.ds(rows - unit, unit), :].astype(F32)
        total = piece if total is None else total + piece
    total = (total * scale).astype(BF16)
    for k in range(everyone):
        total_ref[k] = total


def final_kernel(total_ref, out_ref):
    _, rows, cout = out_ref.shape
    volumes, count, unit, xs = total_ref.shape
    total = total_ref[0].astype(F32)
    for v in range(1, volumes):
        total = total + total_ref[v].astype(F32)
    total = total.reshape(count * unit, xs)
    third = rows // 3
    for at, b in enumerate((2, 0, 1)):
        piece = total[at * third : (at + 1) * third]
        out_ref[2, pl.ds(b * third, third), :] = piece[:, :cout]
        out_ref[0, pl.ds(b * third, third), :] = piece[:, cout:]
    piece = total[3 * third : 4 * third]
    out_ref[1, pl.ds(2 * third, third), :] = piece[:, :cout]
    out_ref[1, pl.ds(0, third), :] = piece[:, cout:]
    piece = total[4 * third : 4 * third + third // 2]
    out_ref[1, pl.ds(third, third // 2), :] = piece[:, :cout]
    out_ref[1, pl.ds(third + third // 2, third // 2), :] = piece[:, cout:]


def near_kernel(recv_ref, k_ref, out_ref, edge_ref, gg_ref, w_ref, t_ref):
    edge_ref[...] = recv_ref[:, 0]
    grads = [recv_ref[:, p] for p in range(recv_ref.shape[1])]
    input_kernel(grads, k_ref, out_ref, gg_ref, w_ref, t_ref)


def far_kernel(recv_ref, halo_ref, k_ref, out_in_ref, out_ref, gg_ref, w_ref, t_ref):
    del out_in_ref
    grads = [recv_ref[:, recv_ref.shape[1] - 1], halo_ref[...]]
    input_kernel(grads, k_ref, out_ref, gg_ref, w_ref, t_ref)


def input_kernel(grads, k_ref, out_ref, gg_ref, w_ref, t_ref):
    cin, planes, ys, xs = out_ref.shape
    blocks, cout, _ = grads[0].shape
    shifts = shift_matrix(xs)

    def shifted(p, here):
        after = jnp.concatenate([here[cout:], jnp.zeros((cout, xs), BF16)], axis=0)
        out = dot(jnp.concatenate([here, after], axis=1), shifts).astype(BF16)
        for k in range(blocks):
            lanes = pl.ds(k * xs, xs)
            rows = slice(k * cout, (k + 1) * cout)
            gg_ref[p, pl.ds(0, cout), lanes] = here[rows]
            for v in range(1, 4):
                gg_ref[p, pl.ds(v * cout, cout), lanes] = out[rows, (v - 1) * xs : v * xs]

    for p, plane in enumerate(grads):
        shifted(p, plane.reshape(blocks * cout, xs))
    for zp in range(2):
        for yp in range(2):
            for xp in range(2):
                for dp in range(2):
                    for dq in range(2):
                        w_ref[
                            pl.ds(((zp * 2 + yp) * 2 + xp) * cin, cin),
                            pl.ds((dp * 2 + dq) * 2 * cout, 2 * cout),
                        ] = weight_block(k_ref, TAP[dp, zp], TAP[dq, yp], xp)
    join = join_matrix(xs)
    weights = w_ref[...]
    group = 4
    width = group * xs

    def one(p, carry):
        for chunk in range(blocks // group):
            lanes = pl.ds(chunk * width, width)
            rhs = gg_ref[pl.ds(p, 2), :, lanes].reshape(8 * cout, width)
            acc = dot(weights, rhs).astype(BF16)
            pairs = []
            for zy in range(4):
                even = acc[zy * 2 * cin : (zy * 2 + 1) * cin]
                odd = acc[(zy * 2 + 1) * cin : (zy * 2 + 2) * cin]
                for kk in range(group):
                    at = slice(kk * xs, (kk + 1) * xs)
                    pairs.append(jnp.concatenate([even[:, at], odd[:, at]], axis=1))
            joined = dot(jnp.concatenate(pairs, axis=0), join)
            for zy in range(4):
                for kk in range(group):
                    at = (zy * group + kk) * cin
                    for h in range(2):
                        y = 4 * (chunk * group + kk) + 2 * h + zy % 2
                        t_ref[zy // 2, pl.ds(y, cin, stride=ys), :] = joined[
                            at : at + cin, h * xs : (h + 1) * xs
                        ]
        for zp in range(2):
            out_ref[:, 2 * p + zp] = t_ref[zp].reshape(cin, ys, xs).astype(BF16)
        return carry

    lax.fori_loop(0, planes // 2, one, 0)


def call(kernel, outs, scratch=(), mib=24, **kwargs):
    return pl.pallas_call(
        kernel,
        out_shape=outs,
        scratch_shapes=scratch,
        compiler_params=pltpu.CompilerParams(vmem_limit_bytes=mib << 20),
        **kwargs,
    )


def stay(value):
    return pltpu.with_memory_space_constraint(value, pltpu.HBM)


HBM = pl.BlockSpec(memory_space=pltpu.HBM)
VMEM = pl.BlockSpec(memory_space=pltpu.VMEM)


def shards(volume, kernel, cotangent):
    count = lax.axis_size("gz")
    everyone = count * lax.axis_size("vol")
    _, cin, planes, ys, xs = volume.shape
    _, cout, ozs, band, oxs = cotangent.shape
    slots = planes // 2
    blocks = ys // 4
    lanes = blocks * xs
    unit = -(-(27 * cin // 2) // (16 * blocks)) * 16
    taps = jnp.transpose(kernel, (2, 3, 4, 1, 0)).reshape(27, cin, cout)

    if band == 2:
        packed, plane = call(
            pack_kernel,
            (
                jax.ShapeDtypeStruct((count, slots, cout, xs), BF16),
                jax.ShapeDtypeStruct((cin, ys, xs), BF16),
            ),
            (
                pltpu.VMEM((4, cout * ozs * band // 4, oxs), BF16),
                pltpu.VMEM((cout * ozs * band // 4, xs), F32),
                pltpu.SemaphoreType.DMA((5,)),
            ),
            in_specs=(HBM, HBM),
            out_specs=(VMEM, VMEM),
        )(stay(cotangent.reshape(cout * ozs * band, oxs)), stay(volume[0]))
    else:
        packed = jnp.transpose(cotangent[0], (1, 0, 2, 3)).reshape(count, slots, cout, band * oxs)
        plane = volume[0, :, planes - 1]
    under = lax.ppermute(plane, "gz", [(i, i + 1) for i in range(count - 1)])
    recv = lax.all_to_all(packed, "gz", 0, 0, tiled=True)
    if band != 2:
        recv = recv.reshape(blocks, 2 // band, slots, cout, band, oxs)
        recv = jnp.transpose(recv, (0, 2, 3, 1, 4, 5)).reshape(blocks, slots, cout, xs)
    xx, mix = call(
        forward_kernel,
        (
            pltpu.HBM((planes + 1, 6 * cin, lanes), BF16),
            pltpu.HBM((blocks, slots * cout + unit, xs), BF16),
        ),
        (
            pltpu.VMEM((planes + 1, 9 * cin, lanes), BF16),
            pltpu.VMEM((cin * ys, xs), F32),
            pltpu.VMEM((2, blocks * cin, 2 * xs), BF16),
            pltpu.SemaphoreType.DMA((planes + 1,)),
        ),
        in_specs=(VMEM, VMEM, VMEM),
        out_specs=(HBM, VMEM),
    )(volume[0], under, taps)
    mix = call(
        weight_kernel,
        pltpu.HBM(mix.shape, BF16),
        (
            pltpu.VMEM((blocks, unit, xs), BF16),
            pltpu.SemaphoreType.DMA,
        ),
        in_specs=(VMEM, VMEM, HBM),
        out_specs=HBM,
        input_output_aliases={2: 0},
    )(recv, xx, stay(mix))
    if band != 2:
        send = mix[:, : slots * cout].reshape(blocks, slots * cout, 2 // band, band * oxs)
        send = jnp.transpose(send, (0, 2, 1, 3)).reshape(count, slots * cout, band * oxs)
        send = jnp.pad(send, ((0, 0), (0, 0), (0, xs - band * oxs)))
        terms = mix[:, slots * cout :].reshape(count, blocks * unit // count, xs)
        mix = jnp.concatenate([send, terms], axis=1)
        unit = terms.shape[1]
    back = lax.all_to_all(mix, "gz", 0, 0, tiled=True)
    volumes = volume.shape[0] * lax.axis_size("vol")

    def add(back_ref, total_ref):
        sum_kernel(back_ref, total_ref, scale=1.0 / volumes)

    total = call(add, jax.ShapeDtypeStruct((everyone, unit, xs), BF16))(back)
    total = lax.all_to_all(total, ("vol", "gz"), 0, 0, tiled=True)
    features = back[:, : slots * cout, : band * oxs].reshape(ozs, cout, band, oxs)
    features = jnp.transpose(features, (1, 0, 2, 3))[None]

    def scratch(slabs):
        return (
            pltpu.VMEM((slabs + 1, 4 * cout, lanes), BF16),
            pltpu.VMEM((8 * cin, 8 * cout), BF16),
            pltpu.VMEM((2, cin * ys, xs), F32),
        )

    whole = pltpu.HBM((cin, planes, ys, xs), BF16)
    volume_grad, edge = call(
        near_kernel,
        (whole, pltpu.HBM((blocks, cout, xs), BF16)),
        scratch(slots - 1),
        grid=(1,),
        in_specs=(VMEM, VMEM),
        out_specs=(
            pl.BlockSpec((cin, planes - 2, ys, xs), lambda i: (0, 0, 0, 0)),
            VMEM,
        ),
    )(recv, taps)
    above = lax.ppermute(edge, "gz", [(i + 1, i) for i in range(count - 1)])
    volume_grad = call(
        far_kernel,
        whole,
        scratch(1),
        grid=(1,),
        in_specs=(VMEM, VMEM, VMEM, HBM),
        out_specs=pl.BlockSpec((cin, 2, ys, xs), lambda i: (0, slots - 1, 0, 0)),
        input_output_aliases={3: 0},
    )(recv, above, taps, stay(volume_grad))[None]

    kernel_grad = call(final_kernel, jax.ShapeDtypeStruct((3, 9 * cin, cout), F32))(
        total.reshape(everyone // count, count, unit, xs)
    )
    kernel_grad = jnp.transpose(kernel_grad.reshape(3, 3, 3, cin, cout), (4, 3, 0, 1, 2))
    return (features, volume_grad, kernel_grad)


def solution(mesh):
    placed = (P("vol", None, "gz", None, None), P(), P("vol", None, None, "gz", None))
    return jax.shard_map(
        shards,
        mesh=mesh,
        in_specs=placed,
        out_specs=(P("vol", None, None, "gz", None), P("vol", None, "gz", None, None), P()),
        check_vma=False,
    )
```

```python
import jax
import jax.numpy as jnp
from jax import lax
from jax.experimental import pallas as pl
from jax.experimental.pallas import tpu as pltpu
from jax.sharding import PartitionSpec as P


F32 = jnp.float32
BF16 = jnp.bfloat16
TAP = {(0, 0): 1, (0, 1): 2, (1, 1): 0, (1, 0): None}


def dot(a, b):
    return lax.dot_general(a, b, (((1,), (0,)), ((), ())), preferred_element_type=F32)


def dot_t(a, b):
    return lax.dot_general(a, b, (((1,), (1,)), ((), ())), preferred_element_type=F32)


def iota(shape, dim):
    return lax.broadcasted_iota(jnp.int32, shape, dim)


def tap_matrix(x, swapped):
    shape = (2 * x, 3 * x)
    row, col = iota(shape, 0), iota(shape, 1)
    half_in, x_in = row // x, row % x
    tap, half_out, r = col // x, (col % x) // (x // 2), col % (x // 2)
    if swapped:
        half_out = 1 - half_out
    hit = (half_in == half_out) & (x_in == 2 * r + tap - 1)
    return jnp.where(hit, 1.0, 0.0).astype(BF16)


def join_matrix(x):
    shape = (2 * x, 2 * x)
    row, col = iota(shape, 0), iota(shape, 1)
    half_in, x_in = col // x, col % x
    parity, half_out, r = row // x, (row % x) // (x // 2), row % (x // 2)
    hit = (half_in == half_out) & (x_in == 2 * r + parity)
    return jnp.where(hit, 1.0, 0.0).astype(BF16)


def shift_matrix(x):
    shape = (2 * x, 3 * x)
    row, col = iota(shape, 0), iota(shape, 1)
    variant, lane = col // x + 1, col % x
    dq, dr = variant // 2, variant % 2
    hit = (row == lane + dq * (x // 2) + dr) & ((dr == 0) | (lane % (x // 2) != x // 2 - 1))
    return jnp.where(hit, 1.0, 0.0).astype(BF16)


def weight_block(k_ref, a, b, xp):
    if a is None or b is None:
        return jnp.zeros((k_ref.shape[1], 2 * k_ref.shape[2]), BF16)
    at = (a * 3 + b) * 3
    if xp == 0:
        one = k_ref[at + 1]
        return jnp.concatenate([one, jnp.zeros_like(one)], axis=1)
    return jnp.concatenate([k_ref[at + 2], k_ref[at]], axis=1)


def pack_kernel(cot_ref, vol_ref, sent_ref, plane_ref, c_ref, s_ref, packed_ref, v_ref, sems):
    parts = c_ref.shape[0]
    take = pltpu.make_async_copy(vol_ref.at[:, vol_ref.shape[1] - 1], v_ref, sems.at[parts])
    give = pltpu.make_async_copy(v_ref, plane_ref, sems.at[parts + 1])
    take.start()
    size = cot_ref.shape[0] // parts
    loads = [
        pltpu.make_async_copy(cot_ref.at[pl.ds(i * size, size)], c_ref.at[i], sems.at[i])
        for i in range(parts)
    ]
    for load in loads:
        load.start()
    count, slots, cout, xs = packed_ref.shape
    half = cot_ref.shape[1]
    own = cout // parts
    stride = size // own
    left = iota((own, xs), 1) < half
    leaves = [
        pltpu.make_async_copy(
            packed_ref.at[:, :, pl.ds(i * own, own)],
            sent_ref.at[:, :, pl.ds(i * own, own)],
            sems.at[parts + 2 + i],
        )
        for i in range(parts)
    ]
    for i in range(parts):
        loads[i].wait()
        s_ref[:, :half] = c_ref[i].astype(F32)
        for p in range(count * slots):
            low = s_ref[pl.ds(2 * p, own, stride=stride), :]
            high = s_ref[pl.ds(2 * p + 1, own, stride=stride), :]
            both = jnp.where(left, low, pltpu.roll(high, half, axis=1))
            packed_ref[p // slots, p % slots, pl.ds(i * own, own)] = both.astype(BF16)
        leaves[i].start()
        if i == 0:
            take.wait()
            give.start()
    for leave in leaves:
        leave.wait()
    give.wait()


def forward_kernel(vol_ref, halo_ref, k_ref, out_ref, mix_ref, xx_ref, t_ref, x_ref, sems):
    cin, planes, ys, xs = vol_ref.shape
    cout = k_ref.shape[2]
    blocks = ys // 4
    split = tap_matrix(xs, False)
    split_swapped = tap_matrix(xs, True)

    def expand(plane, z):
        t_ref[...] = plane.astype(F32).reshape(cin * ys, xs)
        for y in range(ys):
            k, h, yp = y // 4, (y // 2) % 2, y % 2
            rows = t_ref[pl.ds(y, cin, stride=ys), :]
            x_ref[yp, pl.ds(k * cin, cin), pl.ds(h * xs, xs)] = rows.astype(BF16)
        before = jnp.concatenate(
            [jnp.zeros((cin, xs), BF16), x_ref[1, : (blocks - 1) * cin, xs:]], axis=0
        )
        swapped = jnp.concatenate([x_ref[1, :, :xs], before], axis=1)
        for b, (pair, matrix) in enumerate(
            [(swapped, split_swapped), (x_ref[0], split), (x_ref[1], split)]
        ):
            out = dot(pair, matrix).astype(BF16)
            for k in range(blocks):
                for e in range(3):
                    xx_ref[z, pl.ds((b * 3 + e) * cin, cin), pl.ds(k * xs, xs)] = out[
                        k * cin : (k + 1) * cin, e * xs : (e + 1) * xs
                    ]

    def leave(z):
        return pltpu.make_async_copy(
            xx_ref.at[z, pl.ds(3 * cin, 6 * cin)], out_ref.at[z], sems.at[z]
        )

    def own(z, carry):
        expand(vol_ref[:, z], z + 1)
        leave(z + 1).start()
        return carry

    lax.fori_loop(0, planes, own, 0)
    expand(halo_ref[...], 0)
    leave(0).start()
    weights = jnp.transpose(k_ref[...].reshape(27 * cin, cout), (1, 0))
    group = 4
    width = group * xs

    def compute(chunk, carry):
        lanes = pl.ds(pl.multiple_of(chunk * width, width), width)
        for p in range(planes // 2):
            rhs = xx_ref[2 * p : 2 * p + 3, :, lanes].reshape(27 * cin, width)
            value = dot(weights, rhs).astype(BF16)
            for kk in range(group):
                mix_ref[chunk * group + kk, pl.ds(p * cout, cout), :] = value[
                    :, kk * xs : (kk + 1) * xs
                ]
        return carry

    lax.fori_loop(0, blocks // group, compute, 0)
    unit = mix_ref.shape[1] - planes // 2 * cout
    mix_ref[:, pl.ds(planes // 2 * cout, unit), :] = jnp.zeros((blocks, unit, xs), BF16)
    for z in range(planes + 1):
        leave(z).wait()


def weight_kernel(recv_ref, xx_ref, mix_in_ref, mix_ref, part_vmem, sems):
    del mix_in_ref
    blocks, slots, cout, xs = recv_ref.shape
    planes, rows, _ = xx_ref.shape
    count, unit, _ = part_vmem.shape
    third = rows // 2
    grads = [
        jnp.concatenate([recv_ref[k, p] for k in range(blocks)], axis=1) for p in range(slots)
    ]
    nexts = [
        jnp.concatenate([g[:, xs // 2 :], jnp.zeros((cout, xs // 2), BF16)], axis=1)
        for g in grads
    ]
    none = jnp.zeros_like(grads[0])

    def line(*pieces):
        return jnp.concatenate(pieces, axis=1)

    def stack(*pieces):
        return jnp.concatenate(pieces, axis=0)

    def taken(first, at):
        return line(*[xx_ref[z, pl.ds(at, third)] for z in range(first, planes, 2)])

    here = stack(line(none, *grads), line(*grads, none))
    after = stack(line(none, *nexts), line(*nexts, none))
    outer_two = dot_t(taken(0, third), stack(here, after))
    outer_one = dot_t(taken(0, 0), here)
    outer = stack(outer_two[:, : 2 * cout], outer_two[:, 2 * cout :], outer_one).astype(BF16)
    early = rows * 3 // 2 // unit
    ahead = early * unit

    def leave(first, last, sem):
        return pltpu.make_async_copy(
            part_vmem.at[pl.ds(first, last - first)],
            mix_ref.at[pl.ds(first, last - first), pl.ds(slots * cout, unit)],
            sem,
        )

    part_vmem[pl.ds(0, early)] = outer[:ahead].reshape(early, unit, xs)
    leave(0, early, sems.at[0]).start()
    inner_two = dot_t(taken(1, third), stack(line(*grads), line(*nexts)))
    inner_one = dot_t(taken(1, 0), line(*grads))
    part = stack(
        inner_two,
        line(inner_one[: third // 2], inner_one[third // 2 :]),
        jnp.zeros((count * unit - 9 * third // 2, xs), F32),
    ).astype(BF16)
    part = stack(outer[ahead:], part) if ahead < 3 * third else part
    part_vmem[pl.ds(early, count - early)] = part.reshape(count - early, unit, xs)
    leave(early, count, sems.at[1]).start()
    leave(0, early, sems.at[0]).wait()
    leave(early, count, sems.at[1]).wait()


def sum_kernel(back_ref, total_ref, *, scale):
    count, rows, _ = back_ref.shape
    everyone, unit, _ = total_ref.shape
    total = None
    for k in range(count):
        piece = back_ref[k, pl.ds(rows - unit, unit), :].astype(F32)
        total = piece if total is None else total + piece
    total = (total * scale).astype(BF16)
    for k in range(everyone):
        total_ref[k] = total


def final_kernel(total_ref, out_ref):
    _, rows, cout = out_ref.shape
    volumes, count, unit, xs = total_ref.shape
    total = total_ref[0].astype(F32)
    for v in range(1, volumes):
        total = total + total_ref[v].astype(F32)
    total = total.reshape(count * unit, xs)
    third = rows // 3
    for at, b in enumerate((2, 0, 1)):
        piece = total[at * third : (at + 1) * third]
        out_ref[2, pl.ds(b * third, third), :] = piece[:, :cout]
        out_ref[0, pl.ds(b * third, third), :] = piece[:, cout:]
    piece = total[3 * third : 4 * third]
    out_ref[1, pl.ds(2 * third, third), :] = piece[:, :cout]
    out_ref[1, pl.ds(0, third), :] = piece[:, cout:]
    piece = total[4 * third : 4 * third + third // 2]
    out_ref[1, pl.ds(third, third // 2), :] = piece[:, :cout]
    out_ref[1, pl.ds(third + third // 2, third // 2), :] = piece[:, cout:]


def near_kernel(recv_ref, k_ref, out_ref, edge_ref, gg_ref, w_ref, t_ref):
    edge_ref[...] = recv_ref[:, 0]
    grads = [recv_ref[:, p] for p in range(recv_ref.shape[1])]
    input_kernel(grads, k_ref, out_ref, gg_ref, w_ref, t_ref)


def far_kernel(recv_ref, halo_ref, k_ref, out_in_ref, out_ref, gg_ref, w_ref, t_ref):
    del out_in_ref
    grads = [recv_ref[:, recv_ref.shape[1] - 1], halo_ref[...]]
    input_kernel(grads, k_ref, out_ref, gg_ref, w_ref, t_ref)


def input_kernel(grads, k_ref, out_ref, gg_ref, w_ref, t_ref):
    cin, planes, ys, xs = out_ref.shape
    blocks, cout, _ = grads[0].shape
    shifts = shift_matrix(xs)

    def shifted(p, here):
        after = jnp.concatenate([here[cout:], jnp.zeros((cout, xs), BF16)], axis=0)
        out = dot(jnp.concatenate([here, after], axis=1), shifts).astype(BF16)
        for k in range(blocks):
            lanes = pl.ds(k * xs, xs)
            rows = slice(k * cout, (k + 1) * cout)
            gg_ref[p, pl.ds(0, cout), lanes] = here[rows]
            for v in range(1, 4):
                gg_ref[p, pl.ds(v * cout, cout), lanes] = out[rows, (v - 1) * xs : v * xs]

    for p, plane in enumerate(grads):
        shifted(p, plane.reshape(blocks * cout, xs))
    for zp in range(2):
        for yp in range(2):
            for xp in range(2):
                for dp in range(2):
                    for dq in range(2):
                        w_ref[
                            pl.ds(((zp * 2 + yp) * 2 + xp) * cin, cin),
                            pl.ds((dp * 2 + dq) * 2 * cout, 2 * cout),
                        ] = weight_block(k_ref, TAP[dp, zp], TAP[dq, yp], xp)
    join = join_matrix(xs)
    weights = w_ref[...]
    group = 4
    width = group * xs

    def one(p, carry):
        for chunk in range(blocks // group):
            lanes = pl.ds(chunk * width, width)
            rhs = gg_ref[pl.ds(p, 2), :, lanes].reshape(8 * cout, width)
            acc = dot(weights, rhs).astype(BF16)
            pairs = []
            for zy in range(4):
                even = acc[zy * 2 * cin : (zy * 2 + 1) * cin]
                odd = acc[(zy * 2 + 1) * cin : (zy * 2 + 2) * cin]
                for kk in range(group):
                    at = slice(kk * xs, (kk + 1) * xs)
                    pairs.append(jnp.concatenate([even[:, at], odd[:, at]], axis=1))
            joined = dot(jnp.concatenate(pairs, axis=0), join)
            for zy in range(4):
                for kk in range(group):
                    at = (zy * group + kk) * cin
                    for h in range(2):
                        y = 4 * (chunk * group + kk) + 2 * h + zy % 2
                        t_ref[zy // 2, pl.ds(y, cin, stride=ys), :] = joined[
                            at : at + cin, h * xs : (h + 1) * xs
                        ]
        for zp in range(2):
            out_ref[:, 2 * p + zp] = t_ref[zp].reshape(cin, ys, xs).astype(BF16)
        return carry

    lax.fori_loop(0, planes // 2, one, 0)


def call(kernel, outs, scratch=(), mib=24, **kwargs):
    return pl.pallas_call(
        kernel,
        out_shape=outs,
        scratch_shapes=scratch,
        compiler_params=pltpu.CompilerParams(vmem_limit_bytes=mib << 20),
        **kwargs,
    )


def stay(value):
    return pltpu.with_memory_space_constraint(value, pltpu.HBM)


HBM = pl.BlockSpec(memory_space=pltpu.HBM)
VMEM = pl.BlockSpec(memory_space=pltpu.VMEM)


def shards(volume, kernel, cotangent):
    count = lax.axis_size("gz")
    everyone = count * lax.axis_size("vol")
    _, cin, planes, ys, xs = volume.shape
    _, cout, ozs, band, oxs = cotangent.shape
    slots = planes // 2
    blocks = ys // 4
    lanes = blocks * xs
    unit = -(-(27 * cin // 2) // (16 * blocks)) * 16
    taps = jnp.transpose(kernel, (2, 3, 4, 1, 0)).reshape(27, cin, cout)

    if band == 2:
        packed, plane = call(
            pack_kernel,
            (
                pltpu.HBM((count, slots, cout, xs), BF16),
                pltpu.HBM((cin, ys, xs), BF16),
            ),
            (
                pltpu.VMEM((4, cout * ozs * band // 4, oxs), BF16),
                pltpu.VMEM((cout * ozs * band // 4, xs), F32),
                pltpu.VMEM((count, slots, cout, xs), BF16),
                pltpu.VMEM((cin, ys, xs), BF16),
                pltpu.SemaphoreType.DMA((10,)),
            ),
            in_specs=(HBM, HBM),
            out_specs=(HBM, HBM),
        )(stay(cotangent.reshape(cout * ozs * band, oxs)), stay(volume[0]))
    else:
        packed = jnp.transpose(cotangent[0], (1, 0, 2, 3)).reshape(count, slots, cout, band * oxs)
        plane = volume[0, :, planes - 1]
    under = lax.ppermute(plane, "gz", [(i, i + 1) for i in range(count - 1)])
    recv = lax.all_to_all(packed, "gz", 0, 0, tiled=True)
    if band != 2:
        recv = recv.reshape(blocks, 2 // band, slots, cout, band, oxs)
        recv = jnp.transpose(recv, (0, 2, 3, 1, 4, 5)).reshape(blocks, slots, cout, xs)
    xx, mix = call(
        forward_kernel,
        (
            pltpu.HBM((planes + 1, 6 * cin, lanes), BF16),
            pltpu.HBM((blocks, slots * cout + unit, xs), BF16),
        ),
        (
            pltpu.VMEM((planes + 1, 9 * cin, lanes), BF16),
            pltpu.VMEM((cin * ys, xs), F32),
            pltpu.VMEM((2, blocks * cin, 2 * xs), BF16),
            pltpu.SemaphoreType.DMA((planes + 1,)),
        ),
        in_specs=(VMEM, VMEM, VMEM),
        out_specs=(HBM, VMEM),
    )(volume[0], under, taps)
    mix = call(
        weight_kernel,
        pltpu.HBM(mix.shape, BF16),
        (
            pltpu.VMEM((blocks, unit, xs), BF16),
            pltpu.SemaphoreType.DMA((2,)),
        ),
        in_specs=(VMEM, VMEM, HBM),
        out_specs=HBM,
        input_output_aliases={2: 0},
    )(recv, xx, stay(mix))
    if band != 2:
        send = mix[:, : slots * cout].reshape(blocks, slots * cout, 2 // band, band * oxs)
        send = jnp.transpose(send, (0, 2, 1, 3)).reshape(count, slots * cout, band * oxs)
        send = jnp.pad(send, ((0, 0), (0, 0), (0, xs - band * oxs)))
        terms = mix[:, slots * cout :].reshape(count, blocks * unit // count, xs)
        mix = jnp.concatenate([send, terms], axis=1)
        unit = terms.shape[1]
    back = lax.all_to_all(mix, "gz", 0, 0, tiled=True)
    volumes = volume.shape[0] * lax.axis_size("vol")

    def add(back_ref, total_ref):
        sum_kernel(back_ref, total_ref, scale=1.0 / volumes)

    total = call(add, jax.ShapeDtypeStruct((everyone, unit, xs), BF16))(back)
    total = lax.all_to_all(total, ("vol", "gz"), 0, 0, tiled=True)
    features = back[:, : slots * cout, : band * oxs].reshape(ozs, cout, band, oxs)
    features = jnp.transpose(features, (1, 0, 2, 3))[None]

    def scratch(slabs):
        return (
            pltpu.VMEM((slabs + 1, 4 * cout, lanes), BF16),
            pltpu.VMEM((8 * cin, 8 * cout), BF16),
            pltpu.VMEM((2, cin * ys, xs), F32),
        )

    whole = pltpu.HBM((cin, planes, ys, xs), BF16)
    volume_grad, edge = call(
        near_kernel,
        (whole, pltpu.HBM((blocks, cout, xs), BF16)),
        scratch(slots - 1),
        grid=(1,),
        in_specs=(VMEM, VMEM),
        out_specs=(
            pl.BlockSpec((cin, planes - 2, ys, xs), lambda i: (0, 0, 0, 0)),
            VMEM,
        ),
    )(recv, taps)
    above = lax.ppermute(edge, "gz", [(i + 1, i) for i in range(count - 1)])
    volume_grad = call(
        far_kernel,
        whole,
        scratch(1),
        grid=(1,),
        in_specs=(VMEM, VMEM, VMEM, HBM),
        out_specs=pl.BlockSpec((cin, 2, ys, xs), lambda i: (0, slots - 1, 0, 0)),
        input_output_aliases={3: 0},
    )(recv, above, taps, stay(volume_grad))[None]

    kernel_grad = call(final_kernel, jax.ShapeDtypeStruct((3, 9 * cin, cout), F32))(
        total.reshape(everyone // count, count, unit, xs)
    )
    kernel_grad = jnp.transpose(kernel_grad.reshape(3, 3, 3, cin, cout), (4, 3, 0, 1, 2))
    return (features, volume_grad, kernel_grad)


def solution(mesh):
    placed = (P("vol", None, "gz", None, None), P(), P("vol", None, None, "gz", None))
    return jax.shard_map(
        shards,
        mesh=mesh,
        in_specs=placed,
        out_specs=(P("vol", None, None, "gz", None), P("vol", None, "gz", None, None), P()),
        check_vma=False,
    )
```

```python
import jax
import jax.numpy as jnp
from jax import lax
from jax.experimental import pallas as pl
from jax.experimental.pallas import tpu as pltpu
from jax.sharding import PartitionSpec as P


F32 = jnp.float32
BF16 = jnp.bfloat16
TAP = {(0, 0): 1, (0, 1): 2, (1, 1): 0, (1, 0): None}


def dot(a, b):
    return lax.dot_general(a, b, (((1,), (0,)), ((), ())), preferred_element_type=F32)


def dot_t(a, b):
    return lax.dot_general(a, b, (((1,), (1,)), ((), ())), preferred_element_type=F32)


def iota(shape, dim):
    return lax.broadcasted_iota(jnp.int32, shape, dim)


def tap_matrix(x, swapped):
    shape = (2 * x, 3 * x)
    row, col = iota(shape, 0), iota(shape, 1)
    half_in, x_in = row // x, row % x
    tap, half_out, r = col // x, (col % x) // (x // 2), col % (x // 2)
    if swapped:
        half_out = 1 - half_out
    hit = (half_in == half_out) & (x_in == 2 * r + tap - 1)
    return jnp.where(hit, 1.0, 0.0).astype(BF16)


def join_matrix(x):
    shape = (2 * x, 2 * x)
    row, col = iota(shape, 0), iota(shape, 1)
    half_in, x_in = col // x, col % x
    parity, half_out, r = row // x, (row % x) // (x // 2), row % (x // 2)
    hit = (half_in == half_out) & (x_in == 2 * r + parity)
    return jnp.where(hit, 1.0, 0.0).astype(BF16)


def shift_matrix(x):
    shape = (2 * x, 3 * x)
    row, col = iota(shape, 0), iota(shape, 1)
    variant, lane = col // x + 1, col % x
    dq, dr = variant // 2, variant % 2
    hit = (row == lane + dq * (x // 2) + dr) & ((dr == 0) | (lane % (x // 2) != x // 2 - 1))
    return jnp.where(hit, 1.0, 0.0).astype(BF16)


def weight_block(k_ref, a, b, xp):
    if a is None or b is None:
        return jnp.zeros((k_ref.shape[1], 2 * k_ref.shape[2]), BF16)
    at = (a * 3 + b) * 3
    if xp == 0:
        one = k_ref[at + 1]
        return jnp.concatenate([one, jnp.zeros_like(one)], axis=1)
    return jnp.concatenate([k_ref[at + 2], k_ref[at]], axis=1)


def pack_kernel(cot_ref, vol_ref, sent_ref, plane_ref, c_ref, s_ref, m_ref, packed_ref, v_ref, sems):
    parts = c_ref.shape[0]
    take = pltpu.make_async_copy(vol_ref.at[:, vol_ref.shape[1] - 1], v_ref, sems.at[parts])
    give = pltpu.make_async_copy(v_ref, plane_ref, sems.at[parts + 1])
    take.start()
    size = cot_ref.shape[0] // parts
    loads = [
        pltpu.make_async_copy(cot_ref.at[pl.ds(i * size, size)], c_ref.at[i], sems.at[i])
        for i in range(parts)
    ]
    for load in loads:
        load.start()
    count, slots, cout, xs = packed_ref.shape
    half = cot_ref.shape[1]
    own = cout // parts
    stride = size // own
    left = iota((size // 2, xs), 1) < half
    leaves = [
        pltpu.make_async_copy(
            packed_ref.at[:, :, pl.ds(i * own, own)],
            sent_ref.at[:, :, pl.ds(i * own, own)],
            sems.at[parts + 2 + i],
        )
        for i in range(parts)
    ]
    for i in range(parts):
        loads[i].wait()
        s_ref[:, :half] = c_ref[i].astype(F32)
        low = s_ref[pl.ds(0, size // 2, stride=2), :]
        high = s_ref[pl.ds(1, size // 2, stride=2), :]
        m_ref[...] = jnp.where(left, low, pltpu.roll(high, half, axis=1))
        for p in range(count * slots):
            both = m_ref[pl.ds(p, own, stride=stride // 2), :]
            packed_ref[p // slots, p % slots, pl.ds(i * own, own)] = both.astype(BF16)
        leaves[i].start()
        if i == 0:
            take.wait()
            give.start()
    for leave in leaves:
        leave.wait()
    give.wait()


def forward_kernel(vol_ref, halo_ref, k_ref, out_ref, mix_ref, xx_ref, t_ref, x_ref, sems):
    cin, planes, ys, xs = vol_ref.shape
    cout = k_ref.shape[2]
    blocks = ys // 4
    split = tap_matrix(xs, False)
    split_swapped = tap_matrix(xs, True)

    def expand(plane, z):
        t_ref[...] = plane.astype(F32).reshape(cin * ys, xs)
        for y in range(ys):
            k, h, yp = y // 4, (y // 2) % 2, y % 2
            rows = t_ref[pl.ds(y, cin, stride=ys), :]
            x_ref[yp, pl.ds(k * cin, cin), pl.ds(h * xs, xs)] = rows.astype(BF16)
        before = jnp.concatenate(
            [jnp.zeros((cin, xs), BF16), x_ref[1, : (blocks - 1) * cin, xs:]], axis=0
        )
        swapped = jnp.concatenate([x_ref[1, :, :xs], before], axis=1)
        for b, (pair, matrix) in enumerate(
            [(swapped, split_swapped), (x_ref[0], split), (x_ref[1], split)]
        ):
            out = dot(pair, matrix).astype(BF16)
            for k in range(blocks):
                for e in range(3):
                    xx_ref[z, pl.ds((b * 3 + e) * cin, cin), pl.ds(k * xs, xs)] = out[
                        k * cin : (k + 1) * cin, e * xs : (e + 1) * xs
                    ]

    def leave(z):
        return pltpu.make_async_copy(
            xx_ref.at[z, pl.ds(3 * cin, 6 * cin)], out_ref.at[z], sems.at[z]
        )

    def own(z, carry):
        expand(vol_ref[:, z], z + 1)
        leave(z + 1).start()
        return carry

    lax.fori_loop(0, planes, own, 0)
    expand(halo_ref[...], 0)
    leave(0).start()
    weights = jnp.transpose(k_ref[...].reshape(27 * cin, cout), (1, 0))
    group = 4
    width = group * xs

    def compute(chunk, carry):
        lanes = pl.ds(pl.multiple_of(chunk * width, width), width)
        for p in range(planes // 2):
            rhs = xx_ref[2 * p : 2 * p + 3, :, lanes].reshape(27 * cin, width)
            value = dot(weights, rhs).astype(BF16)
            for kk in range(group):
                mix_ref[chunk * group + kk, pl.ds(p * cout, cout), :] = value[
                    :, kk * xs : (kk + 1) * xs
                ]
        return carry

    lax.fori_loop(0, blocks // group, compute, 0)
    unit = mix_ref.shape[1] - planes // 2 * cout
    mix_ref[:, pl.ds(planes // 2 * cout, unit), :] = jnp.zeros((blocks, unit, xs), BF16)
    for z in range(planes + 1):
        leave(z).wait()


def weight_kernel(recv_ref, xx_ref, mix_in_ref, mix_ref, part_vmem, sems):
    del mix_in_ref
    blocks, slots, cout, xs = recv_ref.shape
    planes, rows, _ = xx_ref.shape
    count, unit, _ = part_vmem.shape
    third = rows // 2
    grads = [
        jnp.concatenate([recv_ref[k, p] for k in range(blocks)], axis=1) for p in range(slots)
    ]
    nexts = [
        jnp.concatenate([g[:, xs // 2 :], jnp.zeros((cout, xs // 2), BF16)], axis=1)
        for g in grads
    ]
    none = jnp.zeros_like(grads[0])

    def line(*pieces):
        return jnp.concatenate(pieces, axis=1)

    def stack(*pieces):
        return jnp.concatenate(pieces, axis=0)

    def taken(first, at):
        return line(*[xx_ref[z, pl.ds(at, third)] for z in range(first, planes, 2)])

    here = stack(line(none, *grads), line(*grads, none))
    after = stack(line(none, *nexts), line(*nexts, none))
    outer_two = dot_t(taken(0, third), stack(here, after))
    outer_one = dot_t(taken(0, 0), here)
    outer = stack(outer_two[:, : 2 * cout], outer_two[:, 2 * cout :], outer_one).astype(BF16)
    early = rows * 3 // 2 // unit
    ahead = early * unit

    def leave(first, last, sem):
        return pltpu.make_async_copy(
            part_vmem.at[pl.ds(first, last - first)],
            mix_ref.at[pl.ds(first, last - first), pl.ds(slots * cout, unit)],
            sem,
        )

    part_vmem[pl.ds(0, early)] = outer[:ahead].reshape(early, unit, xs)
    leave(0, early, sems.at[0]).start()
    inner_two = dot_t(taken(1, third), stack(line(*grads), line(*nexts)))
    inner_one = dot_t(taken(1, 0), line(*grads))
    part = stack(
        inner_two,
        line(inner_one[: third // 2], inner_one[third // 2 :]),
        jnp.zeros((count * unit - 9 * third // 2, xs), F32),
    ).astype(BF16)
    part = stack(outer[ahead:], part) if ahead < 3 * third else part
    part_vmem[pl.ds(early, count - early)] = part.reshape(count - early, unit, xs)
    leave(early, count, sems.at[1]).start()
    leave(0, early, sems.at[0]).wait()
    leave(early, count, sems.at[1]).wait()


def sum_kernel(back_ref, total_ref, *, scale):
    count, rows, _ = back_ref.shape
    everyone, unit, _ = total_ref.shape
    total = None
    for k in range(count):
        piece = back_ref[k, pl.ds(rows - unit, unit), :].astype(F32)
        total = piece if total is None else total + piece
    total = (total * scale).astype(BF16)
    for k in range(everyone):
        total_ref[k] = total


def final_kernel(total_ref, out_ref):
    _, rows, cout = out_ref.shape
    volumes, count, unit, xs = total_ref.shape
    total = total_ref[0].astype(F32)
    for v in range(1, volumes):
        total = total + total_ref[v].astype(F32)
    total = total.reshape(count * unit, xs)
    third = rows // 3
    for at, b in enumerate((2, 0, 1)):
        piece = total[at * third : (at + 1) * third]
        out_ref[2, pl.ds(b * third, third), :] = piece[:, :cout]
        out_ref[0, pl.ds(b * third, third), :] = piece[:, cout:]
    piece = total[3 * third : 4 * third]
    out_ref[1, pl.ds(2 * third, third), :] = piece[:, :cout]
    out_ref[1, pl.ds(0, third), :] = piece[:, cout:]
    piece = total[4 * third : 4 * third + third // 2]
    out_ref[1, pl.ds(third, third // 2), :] = piece[:, :cout]
    out_ref[1, pl.ds(third + third // 2, third // 2), :] = piece[:, cout:]


def near_kernel(recv_ref, k_ref, out_ref, edge_ref, gg_ref, w_ref, t_ref):
    edge_ref[...] = recv_ref[:, 0]
    grads = [recv_ref[:, p] for p in range(recv_ref.shape[1])]
    input_kernel(grads, k_ref, out_ref, gg_ref, w_ref, t_ref)


def far_kernel(recv_ref, halo_ref, k_ref, out_in_ref, out_ref, gg_ref, w_ref, t_ref):
    del out_in_ref
    grads = [recv_ref[:, recv_ref.shape[1] - 1], halo_ref[...]]
    input_kernel(grads, k_ref, out_ref, gg_ref, w_ref, t_ref)


def input_kernel(grads, k_ref, out_ref, gg_ref, w_ref, t_ref):
    cin, planes, ys, xs = out_ref.shape
    blocks, cout, _ = grads[0].shape
    shifts = shift_matrix(xs)

    def shifted(p, here):
        after = jnp.concatenate([here[cout:], jnp.zeros((cout, xs), BF16)], axis=0)
        out = dot(jnp.concatenate([here, after], axis=1), shifts).astype(BF16)
        for k in range(blocks):
            lanes = pl.ds(k * xs, xs)
            rows = slice(k * cout, (k + 1) * cout)
            gg_ref[p, pl.ds(0, cout), lanes] = here[rows]
            for v in range(1, 4):
                gg_ref[p, pl.ds(v * cout, cout), lanes] = out[rows, (v - 1) * xs : v * xs]

    for p, plane in enumerate(grads):
        shifted(p, plane.reshape(blocks * cout, xs))
    for zp in range(2):
        for yp in range(2):
            for xp in range(2):
                for dp in range(2):
                    for dq in range(2):
                        w_ref[
                            pl.ds(((zp * 2 + yp) * 2 + xp) * cin, cin),
                            pl.ds((dp * 2 + dq) * 2 * cout, 2 * cout),
                        ] = weight_block(k_ref, TAP[dp, zp], TAP[dq, yp], xp)
    join = join_matrix(xs)
    weights = w_ref[...]
    group = 4
    width = group * xs

    def one(p, carry):
        for chunk in range(blocks // group):
            lanes = pl.ds(chunk * width, width)
            rhs = gg_ref[pl.ds(p, 2), :, lanes].reshape(8 * cout, width)
            acc = dot(weights, rhs).astype(BF16)
            pairs = []
            for zy in range(4):
                even = acc[zy * 2 * cin : (zy * 2 + 1) * cin]
                odd = acc[(zy * 2 + 1) * cin : (zy * 2 + 2) * cin]
                for kk in range(group):
                    at = slice(kk * xs, (kk + 1) * xs)
                    pairs.append(jnp.concatenate([even[:, at], odd[:, at]], axis=1))
            joined = dot(jnp.concatenate(pairs, axis=0), join)
            for zy in range(4):
                for kk in range(group):
                    at = (zy * group + kk) * cin
                    for h in range(2):
                        y = 4 * (chunk * group + kk) + 2 * h + zy % 2
                        t_ref[zy // 2, pl.ds(y, cin, stride=ys), :] = joined[
                            at : at + cin, h * xs : (h + 1) * xs
                        ]
        for zp in range(2):
            out_ref[:, 2 * p + zp] = t_ref[zp].reshape(cin, ys, xs).astype(BF16)
        return carry

    lax.fori_loop(0, planes // 2, one, 0)


def call(kernel, outs, scratch=(), mib=24, **kwargs):
    return pl.pallas_call(
        kernel,
        out_shape=outs,
        scratch_shapes=scratch,
        compiler_params=pltpu.CompilerParams(vmem_limit_bytes=mib << 20),
        **kwargs,
    )


def stay(value):
    return pltpu.with_memory_space_constraint(value, pltpu.HBM)


HBM = pl.BlockSpec(memory_space=pltpu.HBM)
VMEM = pl.BlockSpec(memory_space=pltpu.VMEM)


def shards(volume, kernel, cotangent):
    count = lax.axis_size("gz")
    everyone = count * lax.axis_size("vol")
    _, cin, planes, ys, xs = volume.shape
    _, cout, ozs, band, oxs = cotangent.shape
    slots = planes // 2
    blocks = ys // 4
    lanes = blocks * xs
    unit = -(-(27 * cin // 2) // (16 * blocks)) * 16
    taps = jnp.transpose(kernel, (2, 3, 4, 1, 0)).reshape(27, cin, cout)

    if band == 2:
        packed, plane = call(
            pack_kernel,
            (
                pltpu.HBM((count, slots, cout, xs), BF16),
                pltpu.HBM((cin, ys, xs), BF16),
            ),
            (
                pltpu.VMEM((4, cout * ozs * band // 4, oxs), BF16),
                pltpu.VMEM((cout * ozs * band // 4, xs), F32),
                pltpu.VMEM((cout * ozs * band // 8, xs), F32),
                pltpu.VMEM((count, slots, cout, xs), BF16),
                pltpu.VMEM((cin, ys, xs), BF16),
                pltpu.SemaphoreType.DMA((10,)),
            ),
            in_specs=(HBM, HBM),
            out_specs=(HBM, HBM),
        )(stay(cotangent.reshape(cout * ozs * band, oxs)), stay(volume[0]))
    else:
        packed = jnp.transpose(cotangent[0], (1, 0, 2, 3)).reshape(count, slots, cout, band * oxs)
        plane = volume[0, :, planes - 1]
    under = lax.ppermute(plane, "gz", [(i, i + 1) for i in range(count - 1)])
    recv = lax.all_to_all(packed, "gz", 0, 0, tiled=True)
    if band != 2:
        recv = recv.reshape(blocks, 2 // band, slots, cout, band, oxs)
        recv = jnp.transpose(recv, (0, 2, 3, 1, 4, 5)).reshape(blocks, slots, cout, xs)
    xx, mix = call(
        forward_kernel,
        (
            pltpu.HBM((planes + 1, 6 * cin, lanes), BF16),
            pltpu.HBM((blocks, slots * cout + unit, xs), BF16),
        ),
        (
            pltpu.VMEM((planes + 1, 9 * cin, lanes), BF16),
            pltpu.VMEM((cin * ys, xs), F32),
            pltpu.VMEM((2, blocks * cin, 2 * xs), BF16),
            pltpu.SemaphoreType.DMA((planes + 1,)),
        ),
        in_specs=(VMEM, VMEM, VMEM),
        out_specs=(HBM, VMEM),
    )(volume[0], under, taps)
    mix = call(
        weight_kernel,
        pltpu.HBM(mix.shape, BF16),
        (
            pltpu.VMEM((blocks, unit, xs), BF16),
            pltpu.SemaphoreType.DMA((2,)),
        ),
        in_specs=(VMEM, VMEM, HBM),
        out_specs=HBM,
        input_output_aliases={2: 0},
    )(recv, xx, stay(mix))
    if band != 2:
        send = mix[:, : slots * cout].reshape(blocks, slots * cout, 2 // band, band * oxs)
        send = jnp.transpose(send, (0, 2, 1, 3)).reshape(count, slots * cout, band * oxs)
        send = jnp.pad(send, ((0, 0), (0, 0), (0, xs - band * oxs)))
        terms = mix[:, slots * cout :].reshape(count, blocks * unit // count, xs)
        mix = jnp.concatenate([send, terms], axis=1)
        unit = terms.shape[1]
    back = lax.all_to_all(mix, "gz", 0, 0, tiled=True)
    volumes = volume.shape[0] * lax.axis_size("vol")

    def add(back_ref, total_ref):
        sum_kernel(back_ref, total_ref, scale=1.0 / volumes)

    total = call(add, jax.ShapeDtypeStruct((everyone, unit, xs), BF16))(back)
    total = lax.all_to_all(total, ("vol", "gz"), 0, 0, tiled=True)
    features = back[:, : slots * cout, : band * oxs].reshape(ozs, cout, band, oxs)
    features = jnp.transpose(features, (1, 0, 2, 3))[None]

    def scratch(slabs):
        return (
            pltpu.VMEM((slabs + 1, 4 * cout, lanes), BF16),
            pltpu.VMEM((8 * cin, 8 * cout), BF16),
            pltpu.VMEM((2, cin * ys, xs), F32),
        )

    whole = pltpu.HBM((cin, planes, ys, xs), BF16)
    volume_grad, edge = call(
        near_kernel,
        (whole, pltpu.HBM((blocks, cout, xs), BF16)),
        scratch(slots - 1),
        grid=(1,),
        in_specs=(VMEM, VMEM),
        out_specs=(
            pl.BlockSpec((cin, planes - 2, ys, xs), lambda i: (0, 0, 0, 0)),
            VMEM,
        ),
    )(recv, taps)
    above = lax.ppermute(edge, "gz", [(i + 1, i) for i in range(count - 1)])
    volume_grad = call(
        far_kernel,
        whole,
        scratch(1),
        grid=(1,),
        in_specs=(VMEM, VMEM, VMEM, HBM),
        out_specs=pl.BlockSpec((cin, 2, ys, xs), lambda i: (0, slots - 1, 0, 0)),
        input_output_aliases={3: 0},
    )(recv, above, taps, stay(volume_grad))[None]

    kernel_grad = call(final_kernel, jax.ShapeDtypeStruct((3, 9 * cin, cout), F32))(
        total.reshape(everyone // count, count, unit, xs)
    )
    kernel_grad = jnp.transpose(kernel_grad.reshape(3, 3, 3, cin, cout), (4, 3, 0, 1, 2))
    return (features, volume_grad, kernel_grad)


def solution(mesh):
    placed = (P("vol", None, "gz", None, None), P(), P("vol", None, None, "gz", None))
    return jax.shard_map(
        shards,
        mesh=mesh,
        in_specs=placed,
        out_specs=(P("vol", None, None, "gz", None), P("vol", None, "gz", None, None), P()),
        check_vma=False,
    )
```
